32 devices in a mesh: rep: 2 (over y), seq: 16 (over z, x, core).
Axes of the slice: x: 2, y: 2, z: 4, core: 2. Of those that a mesh axis runs over, the one named last changes fastest.
Arguments:
- tokens: bfloat16 [16384, 768], P(('rep', 'seq')), parts along dimension 0, may hold values from -60 to 60
- w_qkv: bfloat16 [768, 2304], replicated, may hold values from -0.21875 to 0.21875
- w_gate: bfloat16 [768, 36], replicated, may hold values from -0.21875 to 0.21875
- w_out: bfloat16 [768, 768], replicated, may hold values from -0.21875 to 0.21875
- cmp_med: bfloat16 [2, 12, 16], replicated, may hold values from -1.5 to 1.5
- cmp_coarse: bfloat16 [2, 12, 256], replicated, may hold values from -0.375 to 0.375
- group_id: int32 [1024], P('rep'), parts along dimension 0, may hold values from 0 to 7, never falling along the last dimension, each value on 1 to 96 neighbouring positions
Outputs:
- layer_out: bfloat16 [16384, 768], P(('rep', 'seq')), parts along dimension 0
The draws below stay inside these ranges and needn't reach their ends.
There are 2 independent parts, one for each index of `rep`. The reference program is written for one: setup_inputs(seed, part) draws one part's arguments, and reference() takes and returns one part's arrays. A program takes and returns all parts, laid end to end along the dimension named above; an argument that names none is the same for every part. Nothing has to cross between parts.
Inputs may be any that keep to these rules, and one draw needn't show every extreme that they name: `group_id`: never falling along the blocks; each sub-group holds 1 to 96 consecutive blocks, and one holds exactly that many.
All inputs are finite; a program needn't handle non-finite values.
Results may differ from the reference program's by a relative error of at most 0.012.
The reference program's roundings to bfloat16 on the way count: a program that leaves them out, or rounds other values in their place, can miss the bound.
Values may be sent and summed in bfloat16 or wider, within the bound.
A program may use at most 128 MiB of HBM per device.

```python
import math
import jax
import jax.numpy as jnp
import numpy as np
from jax import lax

D = 768
HEADS = 12
HEAD_DIM = 64
TOK_DEV = 512
WINDOW = 128
MED = 16
COARSE = 256
REACH = 3
INNER = 768
TOKENS = 8192
NBLK = 512
N_SEQ = 16


def draw_tokens(key, part):
    values_drawn = jax.random.truncated_normal(key, -6.0, 6.0, (TOKENS, D), jnp.float32)
    return values_drawn.astype(jnp.bfloat16)


def split_up(number_of, total, reach, lean):
    portions = [(1 << 20) // math.isqrt(rank ** lean) + 1 for rank in range(2, number_of + 1)]
    rest, counts = total - reach - (number_of - 1), [1] * (number_of - 1)
    while rest > 0:
        candidates = [i for i in range(number_of - 1) if counts[i] < reach]
        pool, remaining = sum([portions[i] for i in candidates]), rest
        for i in candidates:
            more = min(reach - counts[i], max(1, remaining * portions[i] // pool), rest)
            counts[i] = counts[i] + more
            rest = rest - more
    return np.array([reach] + counts)


def ragged(stream_key, amount, total, limit, slope):
    if amount == 2:
        one = jax.random.randint(stream_key, (), max(1, total - limit), min(limit, total - 1) + 1)
        return jnp.stack([one, total - one])
    lengths = jnp.asarray(split_up(amount, total, limit, slope), jnp.int32)
    couples = (amount - 1) // 2
    giver, receiver = lengths[1:1 + 2 * couples:2], lengths[2:2 + 2 * couples:2]
    room = jnp.minimum(giver - 1, limit - receiver)
    moved = jax.random.randint(jax.random.fold_in(stream_key, 1), (couples,), 0, 1 << 20) % (room + 1)
    lengths = lengths.at[1:1 + 2 * couples:2].set(giver - moved).at[2:2 + 2 * couples:2].set(receiver + moved)
    return lengths[jax.random.permutation(jax.random.fold_in(stream_key, 2), amount)]


def normal_values(own_key, extent, scale, bound, held_as=jnp.bfloat16):
    return jnp.clip(scale * jax.random.normal(own_key, extent, jnp.float32), -bound, bound).astype(held_as)


def setup_inputs(seed: int = 0, part: int = 0) -> dict:
    streams_of = jax.random.split(jax.random.key(seed), 8)
    own_keys = jax.random.split(jax.random.fold_in(streams_of[7], part), 8)
    tokens = draw_tokens(jax.random.fold_in(jax.random.fold_in(streams_of[7], part), 71), part)
    w_qkv = normal_values(streams_of[1], (D, 3 * INNER), D ** -0.5, 0.21875)
    w_gate = normal_values(streams_of[2], (D, 3 * HEADS), D ** -0.5, 0.21875)
    w_out = normal_values(streams_of[3], (INNER, D), INNER ** -0.5, 0.21875)
    cmp_med = normal_values(streams_of[4], (2, HEADS, MED), MED ** -0.5, 1.5)
    cmp_coarse = normal_values(streams_of[5], (2, HEADS, COARSE), COARSE ** -0.5, 0.375)
    group_id = jnp.searchsorted(jnp.cumsum(ragged(own_keys[6], N_SEQ // 2, NBLK, REACH * TOK_DEV // MED, 1)), jnp.arange(NBLK), side="right").astype(jnp.int32)
    return {"tokens": tokens, "w_qkv": w_qkv, "w_gate": w_gate, "w_out": w_out, "cmp_med": cmp_med, "cmp_coarse": cmp_coarse, "group_id": group_id}


def compress(row_data, weights, block_len):
    blocks = row_data.shape[0] // block_len
    shaped = row_data.reshape(blocks, block_len, HEADS, HEAD_DIM).astype(jnp.float32)
    packed = jnp.einsum('bjhd,hj->bhd', shaped, weights.astype(jnp.float32), precision=lax.Precision.HIGHEST)
    return packed.reshape(blocks, HEADS * HEAD_DIM).astype(jnp.bfloat16)


def sink_attend(scores, visible, value_rows):
    masked = jnp.where(visible[:, None, :], scores, -1e30)
    row_peak = jnp.maximum(jnp.max(masked, axis=-1, keepdims=True), 0.0)
    exp_terms = jnp.where(visible[:, None, :], jnp.exp(masked - row_peak), 0.0)
    denominator = jnp.exp(-row_peak) + jnp.sum(exp_terms, axis=-1, keepdims=True)
    weights = (exp_terms / denominator).astype(jnp.bfloat16)
    return jnp.einsum('qhk,khd->qhd', weights.astype(jnp.float32), value_rows.astype(jnp.float32), precision=lax.Precision.HIGHEST)


def reference(tokens, w_qkv, w_gate, w_out, cmp_med, cmp_coarse, group_id):
    inner = HEADS * HEAD_DIM
    scale = HEAD_DIM ** -0.5
    block_rows = min(512, TOK_DEV)
    projected = jnp.dot(tokens, w_qkv, preferred_element_type=jnp.float32).astype(jnp.bfloat16)
    queries = projected[:, :inner]
    key_rows = projected[:, inner:2 * inner]
    value_rows = projected[:, 2 * inner:]
    gate_values = jax.nn.sigmoid(jnp.dot(tokens, w_gate, preferred_element_type=jnp.float32))
    med_keys = compress(key_rows, cmp_med[0], MED)
    med_values = compress(value_rows, cmp_med[1], MED)
    coarse_keys = compress(key_rows, cmp_coarse[0], COARSE).reshape(-1, HEADS, HEAD_DIM)
    coarse_values = compress(value_rows, cmp_coarse[1], COARSE).reshape(-1, HEADS, HEAD_DIM)
    coarse_count = TOKENS // COARSE
    coarse_index = jnp.arange(coarse_count, dtype=jnp.int32)
    padded_keys = jnp.concatenate([jnp.zeros((WINDOW, inner), jnp.bfloat16), key_rows], 0)
    padded_values = jnp.concatenate([jnp.zeros((WINDOW, inner), jnp.bfloat16), value_rows], 0)
    most_blocks = REACH * TOK_DEV // MED
    key_span = most_blocks + block_rows // MED
    total_blocks = TOKENS // MED
    token_groups = jnp.repeat(group_id, MED)

    def one_block(block_index):
        row_start = block_index * block_rows
        query_block = lax.dynamic_slice_in_dim(queries, row_start, block_rows, 0).reshape(block_rows, HEADS, HEAD_DIM).astype(jnp.float32)
        positions = row_start + jnp.arange(block_rows, dtype=jnp.int32)
        win_keys = lax.dynamic_slice_in_dim(padded_keys, row_start, block_rows + WINDOW, 0).reshape(-1, HEADS, HEAD_DIM)
        win_values = lax.dynamic_slice_in_dim(padded_values, row_start, block_rows + WINDOW, 0).reshape(-1, HEADS, HEAD_DIM)
        key_pos = row_start - WINDOW + jnp.arange(block_rows + WINDOW, dtype=jnp.int32)
        visible = (key_pos[None, :] <= positions[:, None]) & (key_pos[None, :] > positions[:, None] - WINDOW) & (key_pos[None, :] >= 0)
        scores = jnp.einsum('qhd,khd->qhk', query_block, win_keys.astype(jnp.float32), precision=lax.Precision.HIGHEST) * scale
        masked = jnp.where(visible[:, None, :], scores, -1e30)
        row_peak = jnp.max(masked, axis=-1, keepdims=True)
        exp_terms = jnp.where(visible[:, None, :], jnp.exp(masked - row_peak), 0.0)
        weights_low = (exp_terms / jnp.sum(exp_terms, axis=-1, keepdims=True)).astype(jnp.bfloat16)
        window_out = jnp.einsum('qhk,khd->qhd', weights_low.astype(jnp.float32), win_values.astype(jnp.float32), precision=lax.Precision.HIGHEST)
        block_first = jnp.clip(row_start // MED - most_blocks, 0, total_blocks - key_span).astype(jnp.int32)
        near_keys = lax.dynamic_slice_in_dim(med_keys, block_first, key_span, 0).reshape(key_span, HEADS, HEAD_DIM)
        near_values = lax.dynamic_slice_in_dim(med_values, block_first, key_span, 0).reshape(key_span, HEADS, HEAD_DIM)
        key_groups = lax.dynamic_slice_in_dim(group_id, block_first, key_span, 0)
        key_blocks = block_first + jnp.arange(key_span, dtype=jnp.int32)
        query_groups = lax.dynamic_slice_in_dim(token_groups, row_start, block_rows, 0)
        visible_med = (key_groups[None, :] == query_groups[:, None]) & (key_blocks[None, :] * MED + MED - 1 <= positions[:, None])
        med_scores = jnp.einsum('qhd,khd->qhk', query_block, near_keys.astype(jnp.float32), precision=lax.Precision.HIGHEST) * scale
        medium_out = sink_attend(med_scores, visible_med, near_values)
        visible_coarse = coarse_index[None, :] * COARSE + COARSE - 1 <= positions[:, None]
        coarse_scores = jnp.einsum('qhd,khd->qhk', query_block, coarse_keys.astype(jnp.float32), precision=lax.Precision.HIGHEST) * scale
        coarse_out = sink_attend(coarse_scores, visible_coarse, coarse_values)
        gate_block = lax.dynamic_slice_in_dim(gate_values, row_start, block_rows, 0)
        mixed_heads = gate_block[:, :HEADS, None] * window_out + gate_block[:, HEADS:2 * HEADS, None] * medium_out + gate_block[:, 2 * HEADS:, None] * coarse_out
        return mixed_heads.reshape(block_rows, inner).astype(jnp.bfloat16)

    mixed_rows = lax.map(one_block, jnp.arange(TOKENS // block_rows, dtype=jnp.int32)).reshape(TOKENS, inner)
    return jnp.dot(mixed_rows, w_out, preferred_element_type=jnp.float32).astype(jnp.bfloat16)
```

```python
import functools
import jax
import jax.numpy as jnp
from jax import lax
from jax.experimental import pallas as pl
from jax.experimental.pallas import tpu as pltpu
from jax.sharding import PartitionSpec as P

WINDOW = 128
REACH = 3
SLOTS = 4
LANES = 128
NEAR = 4
FAR = 256
FRONT = 2
NEG = -1e30
F32 = jnp.float32
BF16 = jnp.bfloat16
MESH = pl.DeviceIdType.MESH


def dot(a, b):
    return jnp.dot(a, b, preferred_element_type=F32)


def dot_t(a, b):
    return lax.dot_general(a, b, (((1,), (1,)), ((), ())), preferred_element_type=F32)


def iota(shape, dim):
    return lax.broadcasted_iota(jnp.int32, shape, dim)


def layer_kernel(
    n_seq, heads, head_dim,
    tok_hbm, wqkv_hbm, wgate_hbm, cmed_hbm, ccoarse_hbm, gid_hbm,
    out_hbm,
    tok, halo, wqkv, wgate, cmed, ccoarse, gid, cmed32, ccoarse32,
    kbuf, vnat, vt, q1, q2, gate_t, bias_m, bias_c, medsend, near, csend, crecv, cf32, mkeys, mvt, ckeys, cvt,
    sbuf, pbuf, fbuf, qbuf, fcbuf, qcbuf, acc, mixed,
    in_sems, out_sems, rim_sems, relay_sems, med_send, med_recv, c_send, c_recv, above,
):
    rows = tok.shape[0]
    inner = heads * head_dim
    pairs = inner // LANES
    per_pair = LANES // head_dim
    med_len = cmed.shape[2]
    coarse_len = ccoarse.shape[2]
    nmed = rows // med_len
    nco = rows // coarse_len
    nblk = gid.shape[1]
    nb = rows // WINDOW
    wide = per_pair * WINDOW
    near_rows = (REACH + 1) * nmed
    scale = head_dim ** (-0.5)
    pos = lax.axis_index("seq")
    rep = lax.axis_index("rep")

    def load(i, src, dst):
        return pltpu.make_async_copy(src, dst, in_sems.at[i])

    loads = [
        load(0, tok_hbm, tok),
        load(1, wqkv_hbm.at[:, inner : 2 * inner], wqkv.at[1]),
        load(2, cmed_hbm, cmed),
        load(3, ccoarse_hbm, ccoarse),
        load(4, wqkv_hbm.at[:, 2 * inner :], wqkv.at[2]),
        load(5, gid_hbm, gid),
        load(6, wqkv_hbm.at[:, :inner], wqkv.at[0]),
        load(7, wgate_hbm, wgate),
    ]
    for copy in loads:
        copy.start()

    near[...] = jnp.zeros(near.shape, BF16)
    crecv[...] = jnp.zeros(crecv.shape, BF16)
    halo[...] = jnp.zeros(halo.shape, BF16)
    mkeys[...] = jnp.zeros(mkeys.shape, BF16)
    mvt[...] = jnp.zeros(mvt.shape, BF16)

    barrier = pltpu.get_barrier_semaphore()

    def greet(j, carry):
        pl.semaphore_signal(barrier, inc=1, device_id=(rep, j), device_id_type=MESH)
        return carry

    lax.fori_loop(jnp.maximum(pos - NEAR, 0), pos, greet, 0)
    lax.fori_loop(pos + 1, jnp.minimum(pos + NEAR + 1, n_seq), greet, 0)
    odd = lax.rem(pos, 2)
    rounds = (n_seq - 2) // NEAR

    loads[2].wait()
    loads[3].wait()
    cmed32[...] = cmed[...].astype(F32)
    ccoarse32[...] = ccoarse[...].astype(F32)
    spread = jnp.where(iota((med_len, rows), 1) % med_len == iota((med_len, rows), 0), 1.0, 0.0)
    spread = spread.astype(BF16)
    in_med = jnp.where(iota((nmed, rows), 1) // med_len == iota((nmed, rows), 0), 1.0, 0.0)
    in_co = jnp.where(iota((8, rows), 1) // coarse_len == iota((8, rows), 0), 1.0, 0.0)
    group = 2 * per_pair
    groups = heads // group
    glanes = 2 * LANES

    def mixers(kv):
        med_w = dot(cmed32[:, kv, :].astype(BF16), spread)
        co_w = jnp.concatenate([ccoarse32[:, kv, :]] * nco, axis=1)
        out = []
        for g in range(groups):
            hs = range(g * group, (g + 1) * group)
            parts = [med_w[h : h + 1, :] * in_med for h in hs]
            parts += [co_w[h : h + 1, :] * in_co for h in hs]
            out.append(jnp.concatenate(parts, axis=0).astype(BF16))
        return out

    lane_head = iota((1, glanes), 1) // head_dim

    def compressed(mixer, block):
        res = dot(mixer, block)
        med = jnp.zeros((nmed, glanes), F32)
        co = jnp.zeros((8, glanes), F32)
        for i in range(group):
            med = jnp.where(lane_head == i, res[i * nmed : (i + 1) * nmed], med)
            base = group * nmed + 8 * i
            co = jnp.where(lane_head == i, res[base : base + 8], co)
        return med, co

    mix = [mixers(0), mixers(1)]
    loads[0].wait()
    co_parts = [[], []]

    def project(kv, g):
        low = dot(tok[...], wqkv[1 + kv, :, g * glanes : (g + 1) * glanes]).astype(BF16)
        for e in range(2):
            cols = slice(e * LANES, (e + 1) * LANES)
            if kv == 0:
                kbuf[2 * g + e, WINDOW:, :] = low[:, cols]
            else:
                vnat[2 * g + e] = low[:, cols]

    def compress(kv, g):
        if kv == 0:
            block = jnp.concatenate([kbuf[2 * g + e, WINDOW:, :] for e in range(2)], axis=1)
        else:
            block = jnp.concatenate([vnat[2 * g + e] for e in range(2)], axis=1)
        med, co = compressed(mix[kv][g], block)
        co_parts[kv].append(co[:nco])
        for e in range(2):
            p = 2 * g + e
            part = med[:, e * LANES : (e + 1) * LANES].astype(BF16)
            medsend[kv * pairs + p] = part
            near[REACH, kv * pairs + p] = part

    def rim_copy():
        return pltpu.make_async_remote_copy(
            src_ref=tok.at[rows - WINDOW :], dst_ref=halo,
            send_sem=rim_sems.at[0], recv_sem=rim_sems.at[1],
            device_id=(rep, lax.rem(pos + 1, n_seq)), device_id_type=MESH,
        )

    def med_copy(kv, d):
        half = slice(kv * pairs, (kv + 1) * pairs)
        return pltpu.make_async_remote_copy(
            src_ref=medsend.at[half], dst_ref=near.at[REACH - d, half],
            send_sem=med_send.at[kv, d - 1], recv_sem=med_recv.at[kv, d - 1],
            device_id=(rep, lax.rem(pos + d, n_seq)), device_id_type=MESH,
        )

    def coarse_copy(d, slot):
        return pltpu.make_async_remote_copy(
            src_ref=csend, dst_ref=crecv.at[slot],
            send_sem=c_send.at[d], recv_sem=c_recv.at[slot],
            device_id=(rep, lax.rem(pos + d, n_seq)), device_id_type=MESH,
        )

    def pass_down():
        pl.semaphore_signal(above, inc=1, device_id=(rep, jnp.maximum(pos - NEAR, 0)), device_id_type=MESH)

    def entered():
        pl.semaphore_wait(barrier, jnp.minimum(pos, NEAR) + jnp.minimum(n_seq - 1 - pos, NEAR))

        @pl.when(pos + 1 < n_seq)
        def _():
            rim_copy().start()

        @pl.when(jnp.logical_and(pos >= NEAR, pos + 1 < n_seq))
        def _():
            pass_down()

    def hear(t):
        more = pos + NEAR * t + 1 < n_seq

        @pl.when(more)
        def _():
            pl.semaphore_wait(above, 1)

        @pl.when(jnp.logical_and(more, pos >= NEAR))
        def _():
            pass_down()

    direct = ((1, odd == 0), (2, True), (3, odd == 1))

    def relay_copy(slot):
        return pltpu.make_async_remote_copy(
            src_ref=near.at[REACH - 2], dst_ref=near.at[slot],
            send_sem=relay_sems.at[0], recv_sem=relay_sems.at[1],
            device_id=(rep, pos + 1 - 2 * odd), device_id_type=MESH,
        )

    def send_medium(kv):
        for d, sends in direct:
            @pl.when(jnp.logical_and(pos + d < n_seq, sends))
            def _(d=d):
                med_copy(kv, d).start()

    steps = [(kv, g) for kv in range(2) for g in range(groups)]
    for k in range(len(steps) + 1):
        if k < len(steps):
            kv, g = steps[k]
            if g == 0:
                loads[1 if kv == 0 else 4].wait()
            project(kv, g)
        if k == 0:
            pl.when(pos >= FRONT)(entered)
        if k == groups:
            pl.when(pos < FRONT)(entered)
        if k > 0:
            compress(*steps[k - 1])
            if steps[k - 1] == (0, groups - 1):
                send_medium(0)
                pl.when(pos >= NEAR)(functools.partial(hear, 1))
    coarse_rows = [jnp.concatenate(parts, axis=1) for parts in co_parts]
    own_coarse = jnp.concatenate(coarse_rows, axis=0).astype(BF16)
    csend[...] = own_coarse
    crecv[pos] = own_coarse

    send_medium(1)

    def send_coarse(d, carry):
        coarse_copy(d, pos).start()
        return carry

    def send_far(t):
        first = NEAR * t + 1
        lax.fori_loop(first, jnp.minimum(first + NEAR, n_seq - pos), send_coarse, 0)

    def hear_and_send(t, carry):
        hear(t)
        send_far(t)
        return carry

    send_far(0)
    pl.when(pos >= NEAR)(functools.partial(send_far, 1))

    loads[6].wait()
    lane = iota((1, LANES), 1) // head_dim
    for g in range(groups):
        full = dot(tok[...], wqkv[0, :, g * glanes : (g + 1) * glanes]) * scale
        for e in range(2):
            part = full[:, e * LANES : (e + 1) * LANES]
            q1[2 * g + e] = part.astype(BF16)
            for h in range(per_pair):
                only = jnp.where(lane == h, part, 0.0).astype(BF16)
                for i in range(nb):
                    q2[2 * g + e, i, h * WINDOW : (h + 1) * WINDOW, :] = only[
                        i * WINDOW : (i + 1) * WINDOW
                    ]
    for p in range(pairs):
        vt[p, :, WINDOW:] = vnat[p].astype(F32).T.astype(BF16)
    loads[7].wait()
    turned = jax.nn.sigmoid(dot_t(wgate[...], tok[...]))
    for level in range(3):
        for h in range(heads):
            row = level * per_pair + h % per_pair
            src = level * heads + h
            gate_t[h // per_pair, row : row + 1, :] = turned[src : src + 1, :]

    loads[5].wait()
    first_blk = (pos - REACH) * nmed
    key_blk = first_blk + iota((near_rows, nblk), 0)
    gid_row = gid[...].astype(F32)
    key_group = jnp.sum(
        jnp.where(iota((near_rows, nblk), 1) == key_blk, gid_row, 0.0), axis=1, keepdims=True
    )
    own_group = key_group[REACH * nmed :]
    tok_group = jnp.sum(in_med * own_group, axis=0, keepdims=True)
    rel_blk = iota((near_rows, rows), 0)
    seen = (
        (key_group == tok_group)
        & ((rel_blk - REACH * nmed) * med_len + med_len - 1 <= iota((near_rows, rows), 1))
        & (rel_blk + first_blk >= 0)
    )
    bias_m[...] = jnp.where(seen, 0.0, NEG)
    krow = iota((n_seq * nco, rows), 0)
    cblk = (krow % n_seq) * nco + krow // n_seq
    seen_c = cblk * coarse_len + coarse_len - 1 <= pos * rows + iota((n_seq * nco, rows), 1)
    bias_c[...] = jnp.where(seen_c, 0.0, NEG)

    older = iota((WINDOW, wide), 0) > iota((WINDOW, wide), 1) % WINDOW
    first_bias = jnp.where(pos == 0, NEG, 0.0).astype(F32)

    def gated(res, level, p, i):
        out = []
        for h in range(per_pair):
            src = level * per_pair + h
            row = gate_t[p, src : src + 1, i * WINDOW : (i + 1) * WINDOW]
            out.append(
                res[h * head_dim : (h + 1) * head_dim, h * WINDOW : (h + 1) * WINDOW] * row
            )
        return jnp.concatenate(out, axis=0)

    def pipelined(units, stages, slots):
        for k in range(len(units) + len(stages) - 1):
            for t, stage in enumerate(stages):
                if 0 <= k - t < len(units):
                    stage(*units[k - t], (k - t) % slots)

    slots = sbuf.shape[0]

    def window_scores(p, i, slot):
        keys = kbuf[p, i * WINDOW : (i + 2) * WINDOW, :]
        scores = dot_t(keys, q2[p, i])
        prev = scores[:WINDOW]
        if i == 0:
            prev = prev + first_bias
        sbuf[slot, :WINDOW] = jnp.where(older, prev, scores[WINDOW:])

    def window_soft(p, i, slot):
        for h in range(per_pair):
            cols = slice(h * WINDOW, (h + 1) * WINDOW)
            both = sbuf[slot, :WINDOW, cols]
            terms = jnp.exp(both - jnp.max(both, axis=0, keepdims=True))
            probs = terms * (1.0 / jnp.sum(terms, axis=0, keepdims=True))
            mask = older[:, cols]
            pbuf[slot, :WINDOW, cols] = jnp.where(mask, probs, 0.0).astype(BF16)
            pbuf[slot, WINDOW:, cols] = jnp.where(mask, 0.0, probs).astype(BF16)

    def window_values(p, i, slot):
        res = dot(vt[p, :, i * WINDOW : (i + 2) * WINDOW], pbuf[slot])
        acc[p, :, i * WINDOW : (i + 1) * WINDOW] = gated(res, 0, p, i)

    window_stages = (window_scores, window_soft, window_values)
    inside = [(p, i) for p in range(pairs) for i in range(1, nb)]
    @pl.when(pos >= NEAR)
    def _():
        hear_and_send(2, 0)

    pipelined(inside, window_stages, slots)

    @pl.when(pos > 0)
    def _():
        rim_copy().wait_recv()

    @pl.when(pos >= 2)
    def _():
        med_copy(0, 2).wait_recv()
        med_copy(1, 2).wait_recv()
        relay_copy(odd * (REACH - 1)).start()

    for kv in range(2):
        for g in range(groups):
            full = dot(halo[...], wqkv[1 + kv, :, g * glanes : (g + 1) * glanes])
            for e in range(2):
                cols = slice(e * LANES, (e + 1) * LANES)
                if kv == 0:
                    kbuf[2 * g + e, :WINDOW, :] = full[:, cols].astype(BF16)
                else:
                    vt[2 * g + e, :, :WINDOW] = full[:, cols].T.astype(BF16)

    lax.fori_loop(jnp.where(pos >= NEAR, 3, 1), rounds + 1, hear_and_send, 0)
    pipelined([(p, 0) for p in range(pairs)], window_stages, slots)

    for d, sender in ((1, odd == 1), (3, odd == 0)):
        @pl.when(jnp.logical_and(pos >= d, sender))
        def _(d=d):
            med_copy(0, d).wait_recv()
            med_copy(1, d).wait_recv()

    @pl.when(pos >= 2)
    def _():
        relay_copy((1 - odd) * (REACH - 1)).wait_recv()

    for p in range(pairs):
        values = jnp.concatenate([near[r, pairs + p] for r in range(REACH + 1)], axis=0)
        turned = values.astype(F32).T.astype(BF16)
        for h in range(per_pair):
            lanes = slice(h * head_dim, (h + 1) * head_dim)
            for r in range(REACH + 1):
                base = h * near_rows + r * nmed
                mkeys[p, base : base + nmed, lanes] = near[r, p, :, lanes]
            mvt[p, lanes, h * near_rows : (h + 1) * near_rows] = turned[lanes, :]

    ncoarse = n_seq * nco
    nf = rows // FAR

    def mix_gate(res, level, p, cols):
        out = []
        for h in range(per_pair):
            row = gate_t[p, level * per_pair + h : level * per_pair + h + 1, cols]
            out.append(res[h * head_dim : (h + 1) * head_dim] * row)
        return jnp.concatenate(out, axis=0)

    def sink_soft(src, dst, slot, count):
        for h in range(per_pair):
            part = slice(h * count, (h + 1) * count)
            scores = src[slot, part]
            peak = jnp.maximum(jnp.max(scores, axis=0, keepdims=True), 0.0)
            terms = jnp.exp(scores - peak)
            total = jnp.exp(-peak) + jnp.sum(terms, axis=0, keepdims=True)
            dst[slot, part] = (terms * (1.0 / total)).astype(BF16)

    def medium_scores(p, i, slot):
        cols = slice(i * FAR, (i + 1) * FAR)
        scores = dot_t(mkeys[p], q1[p, cols, :])
        for h in range(per_pair):
            part = slice(h * near_rows, (h + 1) * near_rows)
            fbuf[slot, part] = scores[part] + bias_m[:, cols]

    def medium_soft(p, i, slot):
        sink_soft(fbuf, qbuf, slot, near_rows)

    def medium_values(p, i, slot):
        cols = slice(i * FAR, (i + 1) * FAR)
        acc[p, :, cols] += mix_gate(dot(mvt[p], qbuf[slot]), 1, p, cols)

    far_units = [(p, i) for p in range(pairs) for i in range(nf)]
    pipelined(far_units, (medium_scores, medium_soft, medium_values), slots)

    def take_coarse(j, carry):
        coarse_copy(1, j).wait_recv()
        return carry

    lax.fori_loop(0, pos, take_coarse, 0)

    def widen(j, carry):
        cf32[j] = crecv[j].astype(F32)
        return carry

    lax.fori_loop(0, n_seq, widen, 0)
    for p in range(pairs):
        cols = slice(p * LANES, (p + 1) * LANES)
        ck = jnp.concatenate([cf32[:, j, cols] for j in range(nco)], axis=0)
        cv = jnp.concatenate([cf32[:, nco + j, cols] for j in range(nco)], axis=0)
        ckeys[p] = jnp.concatenate([jnp.where(lane == h, ck, 0.0) for h in range(per_pair)], axis=0).astype(BF16)
        cv = jnp.concatenate([jnp.where(lane == h, cv, 0.0) for h in range(per_pair)], axis=0)
        cvt[p] = cv.T.astype(BF16)

    def store_pair(p):
        lanes = slice(p * LANES, (p + 1) * LANES)
        return pltpu.make_async_copy(mixed.at[:, lanes], out_hbm.at[:, lanes], out_sems.at[p])

    def coarse_scores(p, i, slot):
        cols = slice(i * FAR, (i + 1) * FAR)
        scores = dot_t(ckeys[p], q1[p, cols, :])
        for h in range(per_pair):
            part = slice(h * ncoarse, (h + 1) * ncoarse)
            fcbuf[slot, part] = scores[part] + bias_c[:, cols]

    def coarse_soft(p, i, slot):
        sink_soft(fcbuf, qcbuf, slot, ncoarse)

    def coarse_values(p, i, slot):
        cols = slice(i * FAR, (i + 1) * FAR)
        total = acc[p, :, cols] + mix_gate(dot(cvt[p], qcbuf[slot]), 2, p, cols)
        mixed[cols, p * LANES : (p + 1) * LANES] = total.T.astype(BF16)
        if i == nf - 1:
            store_pair(p).start()

    pipelined(far_units, (coarse_scores, coarse_soft, coarse_values), slots)

    @pl.when(pos + 1 < n_seq)
    def _():
        rim_copy().wait_send()

    @pl.when(pos >= 2)
    def _():
        relay_copy(odd * (REACH - 1)).wait_send()

    for d, sends in direct:
        @pl.when(jnp.logical_and(pos + d < n_seq, sends))
        def _(d=d):
            med_copy(0, d).wait_send()
            med_copy(1, d).wait_send()

    def sent_coarse(k, carry):
        coarse_copy(k, pos).wait_send()
        return carry

    lax.fori_loop(1, n_seq - pos, sent_coarse, 0)
    for p in range(pairs):
        store_pair(p).wait()


def shards(tokens, w_qkv, w_gate, w_out, cmp_med, cmp_coarse, group_id):
    n_seq = lax.axis_size("seq")
    rows, width = tokens.shape
    heads = cmp_med.shape[1]
    inner = w_out.shape[0]
    head_dim = inner // heads
    med_len, coarse_len = cmp_med.shape[2], cmp_coarse.shape[2]
    nmed, nco = rows // med_len, rows // coarse_len
    pairs = inner // LANES
    per_pair = LANES // head_dim
    nb = rows // WINDOW
    gid = group_id.reshape(1, -1)
    cmed, ccoarse = jnp.swapaxes(cmp_med, 0, 1), jnp.swapaxes(cmp_coarse, 0, 1)
    med_keys = per_pair * (REACH + 1) * nmed
    coarse_keys = per_pair * n_seq * nco
    operands = (tokens, w_qkv, w_gate.T, cmed, ccoarse, gid)
    anywhere = pl.BlockSpec(memory_space=pl.ANY)
    vmem = pltpu.VMEM
    sem = pltpu.SemaphoreType.DMA
    mixed = pl.pallas_call(
        functools.partial(layer_kernel, n_seq, heads, head_dim),
        out_shape=jax.ShapeDtypeStruct((rows, inner), BF16),
        in_specs=[pl.BlockSpec(memory_space=pltpu.HBM)] * 6,
        out_specs=anywhere,
        scratch_shapes=[
            vmem((rows, width), BF16),
            vmem((WINDOW, width), BF16),
            vmem((3, width, inner), BF16),
            vmem(w_gate.shape[::-1], BF16),
            vmem(cmed.shape, BF16),
            vmem(ccoarse.shape, BF16),
            vmem(gid.shape, jnp.int32),
            vmem(cmed.shape, F32),
            vmem(ccoarse.shape, F32),
            vmem((pairs, WINDOW + rows, LANES), BF16),
            vmem((pairs, rows, LANES), BF16),
            vmem((pairs, LANES, WINDOW + rows), BF16),
            vmem((pairs, rows, LANES), BF16),
            vmem((pairs, nb, per_pair * WINDOW, LANES), BF16),
            vmem((pairs, 8, rows), F32),
            vmem(((REACH + 1) * nmed, rows), F32),
            vmem((n_seq * nco, rows), F32),
            vmem((2 * pairs, nmed, LANES), BF16),
            vmem((REACH + 1, 2 * pairs, nmed, LANES), BF16),
            vmem((2 * nco, inner), BF16),
            vmem((n_seq, 2 * nco, inner), BF16),
            vmem((n_seq, 2 * nco, inner), F32),
            vmem((pairs, med_keys, LANES), BF16),
            vmem((pairs, LANES, med_keys), BF16),
            vmem((pairs, coarse_keys, LANES), BF16),
            vmem((pairs, LANES, coarse_keys), BF16),
            vmem((SLOTS, WINDOW, per_pair * WINDOW), F32),
            vmem((SLOTS, 2 * WINDOW, per_pair * WINDOW), BF16),
            vmem((SLOTS, med_keys, FAR), F32),
            vmem((SLOTS, med_keys, FAR), BF16),
            vmem((SLOTS, coarse_keys, FAR), F32),
            vmem((SLOTS, coarse_keys, FAR), BF16),
            vmem((pairs, LANES, rows), F32),
            vmem((rows, inner), BF16),
            sem((8,)),
            sem((pairs,)),
            sem((2,)),
            sem((2,)),
            sem((2, REACH)),
            sem((2, REACH)),
            sem((n_seq,)),
            sem((n_seq,)),
            pltpu.SemaphoreType.REGULAR,
        ],
        compiler_params=pltpu.CompilerParams(
            collective_id=0, has_side_effects=True, vmem_limit_bytes=48 * 1024 * 1024
        ),
        name="sparse_layer",
    )(*[pltpu.with_memory_space_constraint(x, pltpu.HBM) for x in operands])
    return dot(mixed, w_out).astype(BF16)


def solution(mesh):
    placed = (P(("rep", "seq"), None), P(), P(), P(), P(), P(), P("rep"))
    return jax.shard_map(
        shards, mesh=mesh, in_specs=placed, out_specs=P(("rep", "seq"), None), check_vma=False
    )
```

```python
import functools
import jax
import jax.numpy as jnp
from jax import lax
from jax.experimental import pallas as pl
from jax.experimental.pallas import tpu as pltpu
from jax.sharding import PartitionSpec as P

WINDOW = 128
REACH = 3
SLOTS = 3
WINDOW_UNITS = 2
MEDIUM_UNITS = 2
COARSE_UNITS = 6
LANES = 128
NEAR = 4
FAR = 256
FRONT = 2
NEG = -1e30
F32 = jnp.float32
BF16 = jnp.bfloat16
MESH = pl.DeviceIdType.MESH


def dot(a, b):
    return jnp.dot(a, b, preferred_element_type=F32)


def dot_t(a, b):
    return lax.dot_general(a, b, (((1,), (1,)), ((), ())), preferred_element_type=F32)


def iota(shape, dim):
    return lax.broadcasted_iota(jnp.int32, shape, dim)


def layer_kernel(
    n_seq, heads, head_dim,
    tok_hbm, wqkv_hbm, wgate_hbm, cmed_hbm, ccoarse_hbm, gid_hbm,
    out_hbm,
    tok, halo, wqkv, wgate, cmed, ccoarse, gid, cmed32, ccoarse32,
    kbuf, vnat, vt, q1, q2, gate_t, bias_m, bias_c, medsend, near, csend, crecv, cf32, mkeys, mvt, ckeys, cvt,
    sbuf, pbuf, fbuf, qbuf, fcbuf, qcbuf, acc, mixed,
    in_sems, out_sems, rim_sems, relay_sems, med_send, med_recv, c_send, c_recv, above,
):
    rows = tok.shape[0]
    inner = heads * head_dim
    pairs = inner // LANES
    per_pair = LANES // head_dim
    med_len = cmed.shape[2]
    coarse_len = ccoarse.shape[2]
    nmed = rows // med_len
    nco = rows // coarse_len
    nblk = gid.shape[1]
    nb = rows // WINDOW
    wide = per_pair * WINDOW
    near_rows = (REACH + 1) * nmed
    scale = head_dim ** (-0.5)
    pos = lax.axis_index("seq")
    rep = lax.axis_index("rep")

    def load(i, src, dst):
        return pltpu.make_async_copy(src, dst, in_sems.at[i])

    loads = [
        load(0, tok_hbm, tok),
        load(1, wqkv_hbm.at[:, inner : 2 * inner], wqkv.at[1]),
        load(2, cmed_hbm, cmed),
        load(3, ccoarse_hbm, ccoarse),
        load(4, wqkv_hbm.at[:, 2 * inner :], wqkv.at[2]),
        load(5, gid_hbm, gid),
        load(6, wqkv_hbm.at[:, :inner], wqkv.at[0]),
        load(7, wgate_hbm, wgate),
    ]
    for copy in loads:
        copy.start()

    near[...] = jnp.zeros(near.shape, BF16)
    crecv[...] = jnp.zeros(crecv.shape, BF16)
    halo[...] = jnp.zeros(halo.shape, BF16)
    mkeys[...] = jnp.zeros(mkeys.shape, BF16)
    mvt[...] = jnp.zeros(mvt.shape, BF16)

    barrier = pltpu.get_barrier_semaphore()

    def greet(j, carry):
        pl.semaphore_signal(barrier, inc=1, device_id=(rep, j), device_id_type=MESH)
        return carry

    lax.fori_loop(jnp.maximum(pos - NEAR, 0), pos, greet, 0)
    lax.fori_loop(pos + 1, jnp.minimum(pos + NEAR + 1, n_seq), greet, 0)
    odd = lax.rem(pos, 2)
    rounds = (n_seq - 2) // NEAR

    loads[2].wait()
    loads[3].wait()
    cmed32[...] = cmed[...].astype(F32)
    ccoarse32[...] = ccoarse[...].astype(F32)
    spread = jnp.where(iota((med_len, rows), 1) % med_len == iota((med_len, rows), 0), 1.0, 0.0)
    spread = spread.astype(BF16)
    in_med = jnp.where(iota((nmed, rows), 1) // med_len == iota((nmed, rows), 0), 1.0, 0.0)
    in_co = jnp.where(iota((8, rows), 1) // coarse_len == iota((8, rows), 0), 1.0, 0.0)
    group = 2 * per_pair
    groups = heads // group
    glanes = 2 * LANES

    def mixers(kv):
        med_w = dot(cmed32[:, kv, :].astype(BF16), spread)
        co_w = jnp.concatenate([ccoarse32[:, kv, :]] * nco, axis=1)
        out = []
        for g in range(groups):
            hs = range(g * group, (g + 1) * group)
            parts = [med_w[h : h + 1, :] * in_med for h in hs]
            parts += [co_w[h : h + 1, :] * in_co for h in hs]
            out.append(jnp.concatenate(parts, axis=0).astype(BF16))
        return out

    lane_head = iota((1, glanes), 1) // head_dim

    def compressed(mixer, block):
        res = dot(mixer, block)
        med = jnp.zeros((nmed, glanes), F32)
        co = jnp.zeros((8, glanes), F32)
        for i in range(group):
            med = jnp.where(lane_head == i, res[i * nmed : (i + 1) * nmed], med)
            base = group * nmed + 8 * i
            co = jnp.where(lane_head == i, res[base : base + 8], co)
        return med, co

    mix = [mixers(0), mixers(1)]
    co_parts = [[], []]

    def project(kv, g):
        low = dot(tok[...], wqkv[1 + kv, :, g * glanes : (g + 1) * glanes]).astype(BF16)
        for e in range(2):
            cols = slice(e * LANES, (e + 1) * LANES)
            if kv == 0:
                kbuf[2 * g + e, WINDOW:, :] = low[:, cols]
            else:
                vnat[2 * g + e] = low[:, cols]

    def compress(kv, g):
        if kv == 0:
            block = jnp.concatenate([kbuf[2 * g + e, WINDOW:, :] for e in range(2)], axis=1)
        else:
            block = jnp.concatenate([vnat[2 * g + e] for e in range(2)], axis=1)
        med, co = compressed(mix[kv][g], block)
        co_parts[kv].append(co[:nco])
        for e in range(2):
            p = 2 * g + e
            part = med[:, e * LANES : (e + 1) * LANES].astype(BF16)
            medsend[kv * pairs + p] = part
            near[REACH, kv * pairs + p] = part

    def rim_copy():
        return pltpu.make_async_remote_copy(
            src_ref=tok_hbm.at[rows - WINDOW :], dst_ref=halo,
            send_sem=rim_sems.at[0], recv_sem=rim_sems.at[1],
            device_id=(rep, lax.rem(pos + 1, n_seq)), device_id_type=MESH,
        )

    def med_copy(kv, d):
        half = slice(kv * pairs, (kv + 1) * pairs)
        return pltpu.make_async_remote_copy(
            src_ref=medsend.at[half], dst_ref=near.at[REACH - d, half],
            send_sem=med_send.at[kv, d - 1], recv_sem=med_recv.at[kv, d - 1],
            device_id=(rep, lax.rem(pos + d, n_seq)), device_id_type=MESH,
        )

    def coarse_copy(d, slot):
        return pltpu.make_async_remote_copy(
            src_ref=csend, dst_ref=crecv.at[slot],
            send_sem=c_send.at[d], recv_sem=c_recv.at[slot],
            device_id=(rep, lax.rem(pos + d, n_seq)), device_id_type=MESH,
        )

    def pass_down():
        pl.semaphore_signal(above, inc=1, device_id=(rep, jnp.maximum(pos - NEAR, 0)), device_id_type=MESH)

    def entered():
        pl.semaphore_wait(barrier, jnp.minimum(pos, NEAR) + jnp.minimum(n_seq - 1 - pos, NEAR))

        @pl.when(pos + 1 < n_seq)
        def _():
            rim_copy().start()

        @pl.when(jnp.logical_and(pos >= NEAR, pos + 1 < n_seq))
        def _():
            pass_down()

    def hear(t):
        more = pos + NEAR * t + 1 < n_seq

        @pl.when(more)
        def _():
            pl.semaphore_wait(above, 1)

        @pl.when(jnp.logical_and(more, pos >= NEAR))
        def _():
            pass_down()

    direct = ((1, odd == 0), (2, True), (3, odd == 1))

    def relay_copy(kv, slot):
        half = slice(kv * pairs, (kv + 1) * pairs)
        return pltpu.make_async_remote_copy(
            src_ref=near.at[REACH - 2, half], dst_ref=near.at[slot, half],
            send_sem=relay_sems.at[kv, 0], recv_sem=relay_sems.at[kv, 1],
            device_id=(rep, pos + 1 - 2 * odd), device_id_type=MESH,
        )

    def send_medium(kv):
        for d, sends in direct:
            @pl.when(jnp.logical_and(pos + d < n_seq, sends))
            def _(d=d):
                med_copy(kv, d).start()

    pl.when(pos >= FRONT)(entered)
    loads[0].wait()
    steps = [(kv, g) for kv in range(2) for g in range(groups)]
    for k in range(len(steps) + 1):
        if k < len(steps):
            kv, g = steps[k]
            if g == 0:
                loads[1 if kv == 0 else 4].wait()
            project(kv, g)
        if k == groups:
            pl.when(pos < FRONT)(entered)
        if k > 0:
            compress(*steps[k - 1])
            if steps[k - 1] == (0, groups - 1):
                send_medium(0)
                pl.when(pos >= NEAR)(functools.partial(hear, 1))
    coarse_rows = [jnp.concatenate(parts, axis=1) for parts in co_parts]
    own_coarse = jnp.concatenate(coarse_rows, axis=0).astype(BF16)
    csend[...] = own_coarse
    crecv[pos] = own_coarse

    send_medium(1)

    def send_coarse(d, carry):
        coarse_copy(d, pos).start()
        return carry

    def send_far(t):
        first = NEAR * t + 1
        lax.fori_loop(first, jnp.minimum(first + NEAR, n_seq - pos), send_coarse, 0)

    def hear_and_send(t, carry):
        hear(t)
        send_far(t)
        return carry

    send_far(0)
    pl.when(pos >= NEAR)(functools.partial(send_far, 1))

    loads[6].wait()
    loads[7].wait()
    loads[5].wait()
    lane = iota((1, LANES), 1) // head_dim
    for g in range(groups):
        full = dot(tok[...], wqkv[0, :, g * glanes : (g + 1) * glanes]) * scale
        for e in range(2):
            part = full[:, e * LANES : (e + 1) * LANES]
            q1[2 * g + e] = part.astype(BF16)
            for h in range(per_pair):
                only = jnp.where(lane == h, part, 0.0).astype(BF16)
                for i in range(nb):
                    q2[2 * g + e, i, h * WINDOW : (h + 1) * WINDOW, :] = only[
                        i * WINDOW : (i + 1) * WINDOW
                    ]
    for p in range(pairs):
        vt[p, :, WINDOW:] = vnat[p].T
    turned = jax.nn.sigmoid(dot_t(wgate[...], tok[...]))
    for level in range(3):
        for h in range(heads):
            row = level * per_pair + h % per_pair
            src = level * heads + h
            gate_t[h // per_pair, row : row + 1, :] = turned[src : src + 1, :]

    @pl.when(pos >= NEAR)
    def _():
        hear_and_send(2, 0)

    first_blk = (pos - REACH) * nmed
    key_blk = first_blk + iota((near_rows, nblk), 0)
    gid_row = gid[...].astype(F32)
    key_group = jnp.sum(
        jnp.where(iota((near_rows, nblk), 1) == key_blk, gid_row, 0.0), axis=1, keepdims=True
    )
    own_group = key_group[REACH * nmed :]
    tok_group = jnp.sum(in_med * own_group, axis=0, keepdims=True)
    rel_blk = iota((near_rows, rows), 0)
    seen = (
        (key_group == tok_group)
        & ((rel_blk - REACH * nmed) * med_len + med_len - 1 <= iota((near_rows, rows), 1))
        & (rel_blk + first_blk >= 0)
    )
    bias_m[...] = jnp.where(seen, 0.0, NEG)
    krow = iota((n_seq * nco, rows), 0)
    cblk = (krow % n_seq) * nco + krow // n_seq
    seen_c = cblk * coarse_len + coarse_len - 1 <= pos * rows + iota((n_seq * nco, rows), 1)
    bias_c[...] = jnp.where(seen_c, 0.0, NEG)

    older = iota((WINDOW, wide), 0) > iota((WINDOW, wide), 1) % WINDOW
    first_bias = jnp.where(pos == 0, NEG, 0.0).astype(F32)

    def gated(res, level, p, i):
        out = []
        for h in range(per_pair):
            src = level * per_pair + h
            row = gate_t[p, src : src + 1, i * WINDOW : (i + 1) * WINDOW]
            out.append(
                res[h * head_dim : (h + 1) * head_dim, h * WINDOW : (h + 1) * WINDOW] * row
            )
        return jnp.concatenate(out, axis=0)

    def pipelined(units, stages, width, before_last=None):
        batches = [units[a : a + width] for a in range(0, len(units), width)]
        for k in range(len(batches) + len(stages) - 1):
            if before_last is not None and k == len(stages) - 1:
                before_last()
            for t, stage in enumerate(stages):
                if 0 <= k - t < len(batches):
                    for j, unit in enumerate(batches[k - t]):
                        stage(*unit, (k - t) % SLOTS * width + j)


    def window_scores(p, i, slot):
        keys = kbuf[p, i * WINDOW : (i + 2) * WINDOW, :]
        scores = dot_t(keys, q2[p, i])
        prev = scores[:WINDOW]
        if i == 0:
            prev = prev + first_bias
        sbuf[slot, :WINDOW] = jnp.where(older, prev, scores[WINDOW:])

    def window_soft(p, i, slot):
        for h in range(per_pair):
            cols = slice(h * WINDOW, (h + 1) * WINDOW)
            both = sbuf[slot, :WINDOW, cols]
            terms = jnp.exp(both - jnp.max(both, axis=0, keepdims=True))
            probs = terms * (1.0 / jnp.sum(terms, axis=0, keepdims=True))
            mask = older[:, cols]
            pbuf[slot, :WINDOW, cols] = jnp.where(mask, probs, 0.0).astype(BF16)
            pbuf[slot, WINDOW:, cols] = jnp.where(mask, 0.0, probs).astype(BF16)

    def window_values(p, i, slot):
        res = dot(vt[p, :, i * WINDOW : (i + 2) * WINDOW], pbuf[slot])
        acc[p, :, i * WINDOW : (i + 1) * WINDOW] = gated(res, 0, p, i)

    window_stages = (window_scores, window_soft, window_values)
    inside = [(p, i) for p in range(pairs) for i in range(1, nb)]
    pipelined(inside, window_stages, WINDOW_UNITS)

    @pl.when(pos > 0)
    def _():
        rim_copy().wait_recv()

    for kv in range(2):
        for g in range(groups):
            full = dot(halo[...], wqkv[1 + kv, :, g * glanes : (g + 1) * glanes])
            for e in range(2):
                cols = slice(e * LANES, (e + 1) * LANES)
                if kv == 0:
                    kbuf[2 * g + e, :WINDOW, :] = full[:, cols].astype(BF16)
                else:
                    vt[2 * g + e, :, :WINDOW] = full[:, cols].astype(BF16).T

    lax.fori_loop(jnp.where(pos >= NEAR, 3, 1), rounds + 1, hear_and_send, 0)

    def relay(kv):
        @pl.when(pos >= 2)
        def _():
            med_copy(kv, 2).wait_recv()
            relay_copy(kv, odd * (REACH - 1)).start()

    relay(0)
    first = [(p, 0) for p in range(pairs)]
    pipelined(first, window_stages, WINDOW_UNITS, functools.partial(relay, 1))

    def take_medium(kv):
        for d, sender in ((1, odd == 1), (3, odd == 0)):
            @pl.when(jnp.logical_and(pos >= d, sender))
            def _(d=d):
                med_copy(kv, d).wait_recv()

        @pl.when(pos >= 2)
        def _():
            relay_copy(kv, (1 - odd) * (REACH - 1)).wait_recv()

    take_medium(0)
    for p in range(pairs):
        for h in range(per_pair):
            lanes = slice(h * head_dim, (h + 1) * head_dim)
            for r in range(REACH + 1):
                base = h * near_rows + r * nmed
                mkeys[p, base : base + nmed, lanes] = near[r, p, :, lanes]

    def lay_values():
        take_medium(1)
        for p in range(pairs):
            values = jnp.concatenate([near[r, pairs + p] for r in range(REACH + 1)], axis=0)
            turned = values.T
            for h in range(per_pair):
                lanes = slice(h * head_dim, (h + 1) * head_dim)
                mvt[p, lanes, h * near_rows : (h + 1) * near_rows] = turned[lanes, :]

    ncoarse = n_seq * nco
    nf = rows // FAR

    def mix_gate(res, level, p, cols):
        out = []
        for h in range(per_pair):
            row = gate_t[p, level * per_pair + h : level * per_pair + h + 1, cols]
            out.append(res[h * head_dim : (h + 1) * head_dim] * row)
        return jnp.concatenate(out, axis=0)

    def sink_soft(src, dst, slot, count):
        for h in range(per_pair):
            part = slice(h * count, (h + 1) * count)
            scores = src[slot, part]
            peak = jnp.maximum(jnp.max(scores, axis=0, keepdims=True), 0.0)
            terms = jnp.exp(scores - peak)
            total = jnp.exp(-peak) + jnp.sum(terms, axis=0, keepdims=True)
            dst[slot, part] = (terms * (1.0 / total)).astype(BF16)

    def medium_scores(p, i, slot):
        cols = slice(i * FAR, (i + 1) * FAR)
        scores = dot_t(mkeys[p], q1[p, cols, :])
        for h in range(per_pair):
            part = slice(h * near_rows, (h + 1) * near_rows)
            fbuf[slot, part] = scores[part] + bias_m[:, cols]

    def medium_soft(p, i, slot):
        sink_soft(fbuf, qbuf, slot, near_rows)

    def medium_values(p, i, slot):
        cols = slice(i * FAR, (i + 1) * FAR)
        acc[p, :, cols] += mix_gate(dot(mvt[p], qbuf[slot]), 1, p, cols)

    far_units = [(p, i) for p in range(pairs) for i in range(nf)]
    pipelined(far_units, (medium_scores, medium_soft, medium_values), MEDIUM_UNITS, lay_values)

    def take_coarse(j, carry):
        coarse_copy(1, j).wait_recv()
        return carry

    lax.fori_loop(0, pos, take_coarse, 0)

    def widen(j, carry):
        cf32[j] = crecv[j].astype(F32)
        return carry

    lax.fori_loop(0, n_seq, widen, 0)
    for p in range(pairs):
        cols = slice(p * LANES, (p + 1) * LANES)
        ck = jnp.concatenate([cf32[:, j, cols] for j in range(nco)], axis=0)
        cv = jnp.concatenate([cf32[:, nco + j, cols] for j in range(nco)], axis=0)
        ckeys[p] = jnp.concatenate([jnp.where(lane == h, ck, 0.0) for h in range(per_pair)], axis=0).astype(BF16)
        cv = jnp.concatenate([jnp.where(lane == h, cv, 0.0) for h in range(per_pair)], axis=0)
        cvt[p] = cv.T.astype(BF16)

    def store_pair(p):
        lanes = slice(p * LANES, (p + 1) * LANES)
        return pltpu.make_async_copy(mixed.at[:, lanes], out_hbm.at[:, lanes], out_sems.at[p])

    def coarse_scores(p, i, slot):
        cols = slice(i * FAR, (i + 1) * FAR)
        scores = dot_t(ckeys[p], q1[p, cols, :])
        for h in range(per_pair):
            part = slice(h * ncoarse, (h + 1) * ncoarse)
            fcbuf[slot, part] = scores[part] + bias_c[:, cols]

    def coarse_soft(p, i, slot):
        sink_soft(fcbuf, qcbuf, slot, ncoarse)

    def coarse_values(p, i, slot):
        cols = slice(i * FAR, (i + 1) * FAR)
        total = acc[p, :, cols] + mix_gate(dot(cvt[p], qcbuf[slot]), 2, p, cols)
        mixed[cols, p * LANES : (p + 1) * LANES] = total.astype(BF16).T
        if i == nf - 1:
            store_pair(p).start()

    pipelined(far_units, (coarse_scores, coarse_soft, coarse_values), COARSE_UNITS)

    @pl.when(pos + 1 < n_seq)
    def _():
        rim_copy().wait_send()

    @pl.when(pos >= 2)
    def _():
        relay_copy(0, odd * (REACH - 1)).wait_send()
        relay_copy(1, odd * (REACH - 1)).wait_send()

    for d, sends in direct:
        @pl.when(jnp.logical_and(pos + d < n_seq, sends))
        def _(d=d):
            med_copy(0, d).wait_send()
            med_copy(1, d).wait_send()

    def sent_coarse(k, carry):
        coarse_copy(k, pos).wait_send()
        return carry

    lax.fori_loop(1, n_seq - pos, sent_coarse, 0)
    for p in range(pairs):
        store_pair(p).wait()


def shards(tokens, w_qkv, w_gate, w_out, cmp_med, cmp_coarse, group_id):
    n_seq = lax.axis_size("seq")
    rows, width = tokens.shape
    heads = cmp_med.shape[1]
    inner = w_out.shape[0]
    head_dim = inner // heads
    med_len, coarse_len = cmp_med.shape[2], cmp_coarse.shape[2]
    nmed, nco = rows // med_len, rows // coarse_len
    pairs = inner // LANES
    per_pair = LANES // head_dim
    nb = rows // WINDOW
    gid = group_id.reshape(1, -1)
    cmed, ccoarse = jnp.swapaxes(cmp_med, 0, 1), jnp.swapaxes(cmp_coarse, 0, 1)
    med_keys = per_pair * (REACH + 1) * nmed
    coarse_keys = per_pair * n_seq * nco
    operands = (tokens, w_qkv, w_gate.T, cmed, ccoarse, gid)
    anywhere = pl.BlockSpec(memory_space=pl.ANY)
    vmem = pltpu.VMEM
    sem = pltpu.SemaphoreType.DMA
    mixed = pl.pallas_call(
        functools.partial(layer_kernel, n_seq, heads, head_dim),
        out_shape=jax.ShapeDtypeStruct((rows, inner), BF16),
        in_specs=[pl.BlockSpec(memory_space=pltpu.HBM)] * 6,
        out_specs=anywhere,
        scratch_shapes=[
            vmem((rows, width), BF16),
            vmem((WINDOW, width), BF16),
            vmem((3, width, inner), BF16),
            vmem(w_gate.shape[::-1], BF16),
            vmem(cmed.shape, BF16),
            vmem(ccoarse.shape, BF16),
            vmem(gid.shape, jnp.int32),
            vmem(cmed.shape, F32),
            vmem(ccoarse.shape, F32),
            vmem((pairs, WINDOW + rows, LANES), BF16),
            vmem((pairs, rows, LANES), BF16),
            vmem((pairs, LANES, WINDOW + rows), BF16),
            vmem((pairs, rows, LANES), BF16),
            vmem((pairs, nb, per_pair * WINDOW, LANES), BF16),
            vmem((pairs, 8, rows), F32),
            vmem(((REACH + 1) * nmed, rows), F32),
            vmem((n_seq * nco, rows), F32),
            vmem((2 * pairs, nmed, LANES), BF16),
            vmem((REACH + 1, 2 * pairs, nmed, LANES), BF16),
            vmem((2 * nco, inner), BF16),
            vmem((n_seq, 2 * nco, inner), BF16),
            vmem((n_seq, 2 * nco, inner), F32),
            vmem((pairs, med_keys, LANES), BF16),
            vmem((pairs, LANES, med_keys), BF16),
            vmem((pairs, coarse_keys, LANES), BF16),
            vmem((pairs, LANES, coarse_keys), BF16),
            vmem((SLOTS * WINDOW_UNITS, WINDOW, per_pair * WINDOW), F32),
            vmem((SLOTS * WINDOW_UNITS, 2 * WINDOW, per_pair * WINDOW), BF16),
            vmem((SLOTS * MEDIUM_UNITS, med_keys, FAR), F32),
            vmem((SLOTS * MEDIUM_UNITS, med_keys, FAR), BF16),
            vmem((SLOTS * COARSE_UNITS, coarse_keys, FAR), F32),
            vmem((SLOTS * COARSE_UNITS, coarse_keys, FAR), BF16),
            vmem((pairs, LANES, rows), F32),
            vmem((rows, inner), BF16),
            sem((8,)),
            sem((pairs,)),
            sem((2,)),
            sem((2, 2)),
            sem((2, REACH)),
            sem((2, REACH)),
            sem((n_seq,)),
            sem((n_seq,)),
            pltpu.SemaphoreType.REGULAR,
        ],
        compiler_params=pltpu.CompilerParams(
            collective_id=0, has_side_effects=True, vmem_limit_bytes=48 * 1024 * 1024
        ),
        name="sparse_layer",
    )(*[pltpu.with_memory_space_constraint(x, pltpu.HBM) for x in operands])
    return dot(mixed, w_out).astype(BF16)


def solution(mesh):
    placed = (P(("rep", "seq"), None), P(), P(), P(), P(), P(), P("rep"))
    return jax.shard_map(
        shards, mesh=mesh, in_specs=placed, out_specs=P(("rep", "seq"), None), check_vma=False
    )
```

```python
import functools
import jax
import jax.numpy as jnp
from jax import lax
from jax.experimental import pallas as pl
from jax.experimental.pallas import tpu as pltpu
from jax.sharding import PartitionSpec as P

WINDOW = 128
REACH = 3
SLOTS = 4
WINDOW_UNITS = 2
MEDIUM_UNITS = 2
COARSE_UNITS = 6
LANES = 128
NEAR = 4
FAR = 256
FRONT = 2
NEG = -1e30
F32 = jnp.float32
BF16 = jnp.bfloat16
MESH = pl.DeviceIdType.MESH


def dot(a, b):
    return jnp.dot(a, b, preferred_element_type=F32)


def dot_t(a, b):
    return lax.dot_general(a, b, (((1,), (1,)), ((), ())), preferred_element_type=F32)


def iota(shape, dim):
    return lax.broadcasted_iota(jnp.int32, shape, dim)


def layer_kernel(
    n_seq, heads, head_dim,
    tok_hbm, wqkv_hbm, wgate_hbm, cmed_hbm, ccoarse_hbm, gid_hbm, wout_hbm,
    out_hbm,
    tok, halo, wqkv, wgate, wout, cmed, ccoarse, gid, cmed32, ccoarse32,
    kbuf, vnat, vt, q1, q2, gate_t, bias_m, bias_c, medsend, near, csend, crecv, cf32, mkeys, mvt, ckeys, cvt,
    sbuf, pbuf, fbuf, qbuf, fcbuf, qcbuf, acc, mixed, obuf,
    in_sems, out_sems, rim_sems, relay_sems, med_send, med_recv, c_send, c_recv, above,
):
    rows = tok.shape[0]
    inner = heads * head_dim
    pairs = inner // LANES
    per_pair = LANES // head_dim
    med_len = cmed.shape[2]
    coarse_len = ccoarse.shape[2]
    nmed = rows // med_len
    nco = rows // coarse_len
    nblk = gid.shape[1]
    nb = rows // WINDOW
    wide = per_pair * WINDOW
    near_rows = (REACH + 1) * nmed
    scale = head_dim ** (-0.5)
    pos = lax.axis_index("seq")
    rep = lax.axis_index("rep")

    def load(i, src, dst):
        return pltpu.make_async_copy(src, dst, in_sems.at[i])

    loads = [
        load(0, tok_hbm, tok),
        load(1, wqkv_hbm.at[:, inner : 2 * inner], wqkv.at[1]),
        load(2, cmed_hbm, cmed),
        load(3, ccoarse_hbm, ccoarse),
        load(4, wqkv_hbm.at[:, 2 * inner :], wqkv.at[2]),
        load(5, gid_hbm, gid),
        load(6, wqkv_hbm.at[:, :inner], wqkv.at[0]),
        load(7, wgate_hbm, wgate),
        load(8, wout_hbm, wout),
    ]
    for copy in loads:
        copy.start()

    near[...] = jnp.zeros(near.shape, BF16)
    crecv[...] = jnp.zeros(crecv.shape, BF16)
    halo[...] = jnp.zeros(halo.shape, BF16)
    mkeys[...] = jnp.zeros(mkeys.shape, BF16)
    mvt[...] = jnp.zeros(mvt.shape, BF16)

    barrier = pltpu.get_barrier_semaphore()

    def greet(j, carry):
        pl.semaphore_signal(barrier, inc=1, device_id=(rep, j), device_id_type=MESH)
        return carry

    lax.fori_loop(jnp.maximum(pos - NEAR, 0), pos, greet, 0)
    lax.fori_loop(pos + 1, jnp.minimum(pos + NEAR + 1, n_seq), greet, 0)
    odd = lax.rem(pos, 2)
    rounds = (n_seq - 2) // NEAR

    loads[2].wait()
    loads[3].wait()
    cmed32[...] = cmed[...].astype(F32)
    ccoarse32[...] = ccoarse[...].astype(F32)
    spread = jnp.where(iota((med_len, rows), 1) % med_len == iota((med_len, rows), 0), 1.0, 0.0)
    spread = spread.astype(BF16)
    in_med = jnp.where(iota((nmed, rows), 1) // med_len == iota((nmed, rows), 0), 1.0, 0.0)
    in_co = jnp.where(iota((8, rows), 1) // coarse_len == iota((8, rows), 0), 1.0, 0.0)
    group = 2 * per_pair
    groups = heads // group
    glanes = 2 * LANES

    def mixers(kv):
        med_w = dot(cmed32[:, kv, :].astype(BF16), spread)
        co_w = jnp.concatenate([ccoarse32[:, kv, :]] * nco, axis=1)
        out = []
        for g in range(groups):
            hs = range(g * group, (g + 1) * group)
            parts = [med_w[h : h + 1, :] * in_med for h in hs]
            parts += [co_w[h : h + 1, :] * in_co for h in hs]
            out.append(jnp.concatenate(parts, axis=0).astype(BF16))
        return out

    lane_head = iota((1, glanes), 1) // head_dim

    def compressed(mixer, block):
        res = dot(mixer, block)
        med = jnp.zeros((nmed, glanes), F32)
        co = jnp.zeros((8, glanes), F32)
        for i in range(group):
            med = jnp.where(lane_head == i, res[i * nmed : (i + 1) * nmed], med)
            base = group * nmed + 8 * i
            co = jnp.where(lane_head == i, res[base : base + 8], co)
        return med, co

    mix = [mixers(0), mixers(1)]
    co_parts = [[], []]

    def project(kv, g):
        low = dot(tok[...], wqkv[1 + kv, :, g * glanes : (g + 1) * glanes]).astype(BF16)
        for e in range(2):
            cols = slice(e * LANES, (e + 1) * LANES)
            if kv == 0:
                kbuf[2 * g + e, WINDOW:, :] = low[:, cols]
            else:
                vnat[2 * g + e] = low[:, cols]

    def compress(kv, g):
        if kv == 0:
            block = jnp.concatenate([kbuf[2 * g + e, WINDOW:, :] for e in range(2)], axis=1)
        else:
            block = jnp.concatenate([vnat[2 * g + e] for e in range(2)], axis=1)
        med, co = compressed(mix[kv][g], block)
        co_parts[kv].append(co[:nco])
        for e in range(2):
            p = 2 * g + e
            part = med[:, e * LANES : (e + 1) * LANES].astype(BF16)
            medsend[kv * pairs + p] = part
            near[REACH, kv * pairs + p] = part

    def rim_copy():
        return pltpu.make_async_remote_copy(
            src_ref=tok_hbm.at[rows - WINDOW :], dst_ref=halo,
            send_sem=rim_sems.at[0], recv_sem=rim_sems.at[1],
            device_id=(rep, lax.rem(pos + 1, n_seq)), device_id_type=MESH,
        )

    def med_copy(kv, d):
        half = slice(kv * pairs, (kv + 1) * pairs)
        return pltpu.make_async_remote_copy(
            src_ref=medsend.at[half], dst_ref=near.at[REACH - d, half],
            send_sem=med_send.at[kv, d - 1], recv_sem=med_recv.at[kv, d - 1],
            device_id=(rep, lax.rem(pos + d, n_seq)), device_id_type=MESH,
        )

    def coarse_copy(d, slot):
        return pltpu.make_async_remote_copy(
            src_ref=csend, dst_ref=crecv.at[slot],
            send_sem=c_send.at[d], recv_sem=c_recv.at[slot],
            device_id=(rep, lax.rem(pos + d, n_seq)), device_id_type=MESH,
        )

    def pass_down():
        pl.semaphore_signal(above, inc=1, device_id=(rep, jnp.maximum(pos - NEAR, 0)), device_id_type=MESH)

    def entered():
        pl.semaphore_wait(barrier, jnp.minimum(pos, NEAR) + jnp.minimum(n_seq - 1 - pos, NEAR))

        @pl.when(pos + 1 < n_seq)
        def _():
            rim_copy().start()

        @pl.when(jnp.logical_and(pos >= NEAR, pos + 1 < n_seq))
        def _():
            pass_down()

    def hear(t):
        more = pos + NEAR * t + 1 < n_seq

        @pl.when(more)
        def _():
            pl.semaphore_wait(above, 1)

        @pl.when(jnp.logical_and(more, pos >= NEAR))
        def _():
            pass_down()

    direct = ((1, odd == 0), (2, True), (3, odd == 1))

    def relay_copy(kv, slot):
        half = slice(kv * pairs, (kv + 1) * pairs)
        return pltpu.make_async_remote_copy(
            src_ref=near.at[REACH - 2, half], dst_ref=near.at[slot, half],
            send_sem=relay_sems.at[kv, 0], recv_sem=relay_sems.at[kv, 1],
            device_id=(rep, pos + 1 - 2 * odd), device_id_type=MESH,
        )

    def send_medium(kv):
        for d, sends in direct:
            @pl.when(jnp.logical_and(pos + d < n_seq, sends))
            def _(d=d):
                med_copy(kv, d).start()

    pl.when(pos >= FRONT)(entered)
    loads[0].wait()
    steps = [(kv, g) for kv in range(2) for g in range(groups)]
    for k in range(len(steps) + 1):
        if k < len(steps):
            kv, g = steps[k]
            if g == 0:
                loads[1 if kv == 0 else 4].wait()
            project(kv, g)
        if k == groups:
            pl.when(pos < FRONT)(entered)
        if k > 0:
            compress(*steps[k - 1])
            if steps[k - 1] == (0, groups - 1):
                send_medium(0)
                pl.when(pos >= NEAR)(functools.partial(hear, 1))
    coarse_rows = [jnp.concatenate(parts, axis=1) for parts in co_parts]
    own_coarse = jnp.concatenate(coarse_rows, axis=0).astype(BF16)
    csend[...] = own_coarse
    crecv[pos] = own_coarse

    send_medium(1)

    def send_coarse(d, carry):
        coarse_copy(d, pos).start()
        return carry

    def send_far(t):
        first = NEAR * t + 1
        lax.fori_loop(first, jnp.minimum(first + NEAR, n_seq - pos), send_coarse, 0)

    def hear_and_send(t, carry):
        hear(t)
        send_far(t)
        return carry

    send_far(0)
    pl.when(pos >= NEAR)(functools.partial(send_far, 1))

    loads[6].wait()
    loads[7].wait()
    loads[5].wait()
    lane = iota((1, LANES), 1) // head_dim
    for g in range(groups):
        full = dot(tok[...], wqkv[0, :, g * glanes : (g + 1) * glanes]) * scale
        for e in range(2):
            part = full[:, e * LANES : (e + 1) * LANES]
            q1[2 * g + e] = part.astype(BF16)
            for h in range(per_pair):
                only = jnp.where(lane == h, part, 0.0).astype(BF16)
                for i in range(nb):
                    q2[2 * g + e, i, h * WINDOW : (h + 1) * WINDOW, :] = only[
                        i * WINDOW : (i + 1) * WINDOW
                    ]
    for p in range(pairs):
        vt[p, :, WINDOW:] = vnat[p].T
    turned = jax.nn.sigmoid(dot_t(wgate[...], tok[...]))
    for level in range(3):
        for h in range(heads):
            row = level * per_pair + h % per_pair
            src = level * heads + h
            gate_t[h // per_pair, row : row + 1, :] = turned[src : src + 1, :]

    @pl.when(pos >= NEAR)
    def _():
        hear_and_send(2, 0)

    first_blk = (pos - REACH) * nmed
    key_blk = first_blk + iota((near_rows, nblk), 0)
    gid_row = gid[...].astype(F32)
    key_group = jnp.sum(
        jnp.where(iota((near_rows, nblk), 1) == key_blk, gid_row, 0.0), axis=1, keepdims=True
    )
    own_group = key_group[REACH * nmed :]
    tok_group = jnp.sum(in_med * own_group, axis=0, keepdims=True)
    rel_blk = iota((near_rows, rows), 0)
    seen = (
        (key_group == tok_group)
        & ((rel_blk - REACH * nmed) * med_len + med_len - 1 <= iota((near_rows, rows), 1))
        & (rel_blk + first_blk >= 0)
    )
    bias_m[...] = jnp.where(seen, 0.0, NEG)
    krow = iota((n_seq * nco, rows), 0)
    cblk = (krow % n_seq) * nco + krow // n_seq
    seen_c = cblk * coarse_len + coarse_len - 1 <= pos * rows + iota((n_seq * nco, rows), 1)
    bias_c[...] = jnp.where(seen_c, 0.0, NEG)

    older = iota((WINDOW, wide), 0) > iota((WINDOW, wide), 1) % WINDOW
    first_bias = jnp.where(pos == 0, NEG, 0.0).astype(F32)

    def gated(res, level, p, i):
        out = []
        for h in range(per_pair):
            src = level * per_pair + h
            row = gate_t[p, src : src + 1, i * WINDOW : (i + 1) * WINDOW]
            out.append(
                res[h * head_dim : (h + 1) * head_dim, h * WINDOW : (h + 1) * WINDOW] * row
            )
        return jnp.concatenate(out, axis=0)

    def pipelined(units, stages, width, before_last=None):
        batches = [units[a : a + width] for a in range(0, len(units), width)]
        for k in range(len(batches) + len(stages) - 1):
            if before_last is not None and k == len(stages) - 1:
                before_last()
            for t, stage in enumerate(stages):
                if 0 <= k - t < len(batches):
                    for j, unit in enumerate(batches[k - t]):
                        stage(*unit, (k - t) % SLOTS * width + j)


    def window_scores(p, i, slot):
        keys = kbuf[p, i * WINDOW : (i + 2) * WINDOW, :]
        scores = dot_t(keys, q2[p, i])
        prev = scores[:WINDOW]
        if i == 0:
            prev = prev + first_bias
        sbuf[slot, :WINDOW] = jnp.where(older, prev, scores[WINDOW:])

    def window_soft(p, i, slot):
        for h in range(per_pair):
            cols = slice(h * WINDOW, (h + 1) * WINDOW)
            both = sbuf[slot, :WINDOW, cols]
            terms = jnp.exp(both - jnp.max(both, axis=0, keepdims=True))
            probs = terms * (1.0 / jnp.sum(terms, axis=0, keepdims=True))
            mask = older[:, cols]
            pbuf[slot, :WINDOW, cols] = jnp.where(mask, probs, 0.0).astype(BF16)
            pbuf[slot, WINDOW:, cols] = jnp.where(mask, 0.0, probs).astype(BF16)

    def window_values(p, i, slot):
        res = dot(vt[p, :, i * WINDOW : (i + 2) * WINDOW], pbuf[slot])
        acc[p, :, i * WINDOW : (i + 1) * WINDOW] = gated(res, 0, p, i)

    window_stages = (window_scores, window_soft, window_values)
    inside = [(p, i) for p in range(pairs) for i in range(1, nb)]
    pipelined(inside, window_stages, WINDOW_UNITS)

    @pl.when(pos > 0)
    def _():
        rim_copy().wait_recv()

    for kv in range(2):
        for g in range(groups):
            full = dot(halo[...], wqkv[1 + kv, :, g * glanes : (g + 1) * glanes])
            for e in range(2):
                cols = slice(e * LANES, (e + 1) * LANES)
                if kv == 0:
                    kbuf[2 * g + e, :WINDOW, :] = full[:, cols].astype(BF16)
                else:
                    vt[2 * g + e, :, :WINDOW] = full[:, cols].astype(BF16).T

    lax.fori_loop(jnp.where(pos >= NEAR, 3, 1), rounds + 1, hear_and_send, 0)

    def relay(kv):
        @pl.when(pos >= 2)
        def _():
            med_copy(kv, 2).wait_recv()
            relay_copy(kv, odd * (REACH - 1)).start()

    relay(0)
    first = [(p, 0) for p in range(pairs)]
    pipelined(first, window_stages, WINDOW_UNITS, functools.partial(relay, 1))

    def take_medium(kv):
        for d, sender in ((1, odd == 1), (3, odd == 0)):
            @pl.when(jnp.logical_and(pos >= d, sender))
            def _(d=d):
                med_copy(kv, d).wait_recv()

        @pl.when(pos >= 2)
        def _():
            relay_copy(kv, (1 - odd) * (REACH - 1)).wait_recv()

    take_medium(0)
    for p in range(pairs):
        for h in range(per_pair):
            lanes = slice(h * head_dim, (h + 1) * head_dim)
            for r in range(REACH + 1):
                base = h * near_rows + r * nmed
                mkeys[p, base : base + nmed, lanes] = near[r, p, :, lanes]

    def lay_values():
        take_medium(1)
        for p in range(pairs):
            values = jnp.concatenate([near[r, pairs + p] for r in range(REACH + 1)], axis=0)
            turned = values.T
            for h in range(per_pair):
                lanes = slice(h * head_dim, (h + 1) * head_dim)
                mvt[p, lanes, h * near_rows : (h + 1) * near_rows] = turned[lanes, :]

    ncoarse = n_seq * nco
    nf = rows // FAR

    def mix_gate(res, level, p, cols):
        out = []
        for h in range(per_pair):
            row = gate_t[p, level * per_pair + h : level * per_pair + h + 1, cols]
            out.append(res[h * head_dim : (h + 1) * head_dim] * row)
        return jnp.concatenate(out, axis=0)

    def sink_soft(src, dst, slot, count):
        for h in range(per_pair):
            part = slice(h * count, (h + 1) * count)
            scores = src[slot, part]
            peak = jnp.maximum(jnp.max(scores, axis=0, keepdims=True), 0.0)
            terms = jnp.exp(scores - peak)
            total = jnp.exp(-peak) + jnp.sum(terms, axis=0, keepdims=True)
            dst[slot, part] = (terms * (1.0 / total)).astype(BF16)

    def medium_scores(p, i, slot):
        cols = slice(i * FAR, (i + 1) * FAR)
        scores = dot_t(mkeys[p], q1[p, cols, :])
        for h in range(per_pair):
            part = slice(h * near_rows, (h + 1) * near_rows)
            fbuf[slot, part] = scores[part] + bias_m[:, cols]

    def medium_soft(p, i, slot):
        sink_soft(fbuf, qbuf, slot, near_rows)

    def medium_values(p, i, slot):
        cols = slice(i * FAR, (i + 1) * FAR)
        acc[p, :, cols] += mix_gate(dot(mvt[p], qbuf[slot]), 1, p, cols)

    far_units = [(p, i) for p in range(pairs) for i in range(nf)]
    pipelined(far_units, (medium_scores, medium_soft, medium_values), MEDIUM_UNITS, lay_values)

    def take_coarse(j, carry):
        coarse_copy(1, j).wait_recv()
        return carry

    lax.fori_loop(0, pos, take_coarse, 0)

    def widen(j, carry):
        cf32[j] = crecv[j].astype(F32)
        return carry

    lax.fori_loop(0, n_seq, widen, 0)
    for p in range(pairs):
        cols = slice(p * LANES, (p + 1) * LANES)
        ck = jnp.concatenate([cf32[:, j, cols] for j in range(nco)], axis=0)
        cv = jnp.concatenate([cf32[:, nco + j, cols] for j in range(nco)], axis=0)
        ckeys[p] = jnp.concatenate([jnp.where(lane == h, ck, 0.0) for h in range(per_pair)], axis=0).astype(BF16)
        cv = jnp.concatenate([jnp.where(lane == h, cv, 0.0) for h in range(per_pair)], axis=0)
        cvt[p] = cv.T.astype(BF16)

    def store_rows(i):
        part = slice(i * FAR, (i + 1) * FAR)
        return pltpu.make_async_copy(obuf.at[part], out_hbm.at[part], out_sems.at[i])

    def coarse_scores(p, i, slot):
        cols = slice(i * FAR, (i + 1) * FAR)
        scores = dot_t(ckeys[p], q1[p, cols, :])
        for h in range(per_pair):
            part = slice(h * ncoarse, (h + 1) * ncoarse)
            fcbuf[slot, part] = scores[part] + bias_c[:, cols]

    def coarse_soft(p, i, slot):
        sink_soft(fcbuf, qcbuf, slot, ncoarse)

    def coarse_values(p, i, slot):
        cols = slice(i * FAR, (i + 1) * FAR)
        total = acc[p, :, cols] + mix_gate(dot(cvt[p], qcbuf[slot]), 2, p, cols)
        mixed[cols, p * LANES : (p + 1) * LANES] = total.astype(BF16).T

    def project_out(p, i, slot):
        if p == pairs - 1:
            part = slice(i * FAR, (i + 1) * FAR)
            obuf[part] = dot(mixed[part], wout[...]).astype(BF16)
            store_rows(i).start()

    loads[8].wait()
    by_rows = [(p, i) for i in range(nf) for p in range(pairs)]
    pipelined(by_rows, (coarse_scores, coarse_soft, coarse_values, project_out), COARSE_UNITS)

    @pl.when(pos + 1 < n_seq)
    def _():
        rim_copy().wait_send()

    @pl.when(pos >= 2)
    def _():
        relay_copy(0, odd * (REACH - 1)).wait_send()
        relay_copy(1, odd * (REACH - 1)).wait_send()

    for d, sends in direct:
        @pl.when(jnp.logical_and(pos + d < n_seq, sends))
        def _(d=d):
            med_copy(0, d).wait_send()
            med_copy(1, d).wait_send()

    def sent_coarse(k, carry):
        coarse_copy(k, pos).wait_send()
        return carry

    lax.fori_loop(1, n_seq - pos, sent_coarse, 0)
    for i in range(nf):
        store_rows(i).wait()


def shards(tokens, w_qkv, w_gate, w_out, cmp_med, cmp_coarse, group_id):
    n_seq = lax.axis_size("seq")
    rows, width = tokens.shape
    heads = cmp_med.shape[1]
    inner = w_out.shape[0]
    head_dim = inner // heads
    med_len, coarse_len = cmp_med.shape[2], cmp_coarse.shape[2]
    nmed, nco = rows // med_len, rows // coarse_len
    pairs = inner // LANES
    per_pair = LANES // head_dim
    nb = rows // WINDOW
    gid = group_id.reshape(1, -1)
    cmed, ccoarse = jnp.swapaxes(cmp_med, 0, 1), jnp.swapaxes(cmp_coarse, 0, 1)
    med_keys = per_pair * (REACH + 1) * nmed
    coarse_keys = per_pair * n_seq * nco
    operands = (tokens, w_qkv, w_gate.T, cmed, ccoarse, gid, w_out)
    anywhere = pl.BlockSpec(memory_space=pl.ANY)
    vmem = pltpu.VMEM
    sem = pltpu.SemaphoreType.DMA
    return pl.pallas_call(
        functools.partial(layer_kernel, n_seq, heads, head_dim),
        out_shape=jax.ShapeDtypeStruct((rows, w_out.shape[1]), BF16),
        in_specs=[pl.BlockSpec(memory_space=pltpu.HBM)] * 7,
        out_specs=anywhere,
        scratch_shapes=[
            vmem((rows, width), BF16),
            vmem((WINDOW, width), BF16),
            vmem((3, width, inner), BF16),
            vmem(w_gate.shape[::-1], BF16),
            vmem(w_out.shape, BF16),
            vmem(cmed.shape, BF16),
            vmem(ccoarse.shape, BF16),
            vmem(gid.shape, jnp.int32),
            vmem(cmed.shape, F32),
            vmem(ccoarse.shape, F32),
            vmem((pairs, WINDOW + rows, LANES), BF16),
            vmem((pairs, rows, LANES), BF16),
            vmem((pairs, LANES, WINDOW + rows), BF16),
            vmem((pairs, rows, LANES), BF16),
            vmem((pairs, nb, per_pair * WINDOW, LANES), BF16),
            vmem((pairs, 8, rows), F32),
            vmem(((REACH + 1) * nmed, rows), F32),
            vmem((n_seq * nco, rows), F32),
            vmem((2 * pairs, nmed, LANES), BF16),
            vmem((REACH + 1, 2 * pairs, nmed, LANES), BF16),
            vmem((2 * nco, inner), BF16),
            vmem((n_seq, 2 * nco, inner), BF16),
            vmem((n_seq, 2 * nco, inner), F32),
            vmem((pairs, med_keys, LANES), BF16),
            vmem((pairs, LANES, med_keys), BF16),
            vmem((pairs, coarse_keys, LANES), BF16),
            vmem((pairs, LANES, coarse_keys), BF16),
            vmem((SLOTS * WINDOW_UNITS, WINDOW, per_pair * WINDOW), F32),
            vmem((SLOTS * WINDOW_UNITS, 2 * WINDOW, per_pair * WINDOW), BF16),
            vmem((SLOTS * MEDIUM_UNITS, med_keys, FAR), F32),
            vmem((SLOTS * MEDIUM_UNITS, med_keys, FAR), BF16),
            vmem((SLOTS * COARSE_UNITS, coarse_keys, FAR), F32),
            vmem((SLOTS * COARSE_UNITS, coarse_keys, FAR), BF16),
            vmem((pairs, LANES, rows), F32),
            vmem((rows, inner), BF16),
            vmem((rows, w_out.shape[1]), BF16),
            sem((9,)),
            sem((rows // FAR,)),
            sem((2,)),
            sem((2, 2)),
            sem((2, REACH)),
            sem((2, REACH)),
            sem((n_seq,)),
            sem((n_seq,)),
            pltpu.SemaphoreType.REGULAR,
        ],
        compiler_params=pltpu.CompilerParams(
            collective_id=0, has_side_effects=True, vmem_limit_bytes=48 * 1024 * 1024
        ),
        name="sparse_layer",
    )(*[pltpu.with_memory_space_constraint(x, pltpu.HBM) for x in operands])


def solution(mesh):
    placed = (P(("rep", "seq"), None), P(), P(), P(), P(), P(), P("rep"))
    return jax.shard_map(
        shards, mesh=mesh, in_specs=placed, out_specs=P(("rep", "seq"), None), check_vma=False
    )
```

```python
import functools
import jax
import jax.numpy as jnp
from jax import lax
from jax.experimental import pallas as pl
from jax.experimental.pallas import tpu as pltpu
from jax.sharding import PartitionSpec as P

WINDOW = 128
REACH = 3
SLOTS = 4
WINDOW_UNITS = 2
MEDIUM_UNITS = 2
COARSE_UNITS = 6
LANES = 128
NEAR = 4
FAR = 256
FRONT = 2
NEG = -1e30
F32 = jnp.float32
BF16 = jnp.bfloat16
MESH = pl.DeviceIdType.MESH


def dot(a, b):
    return jnp.dot(a, b, preferred_element_type=F32)


def dot_t(a, b):
    return lax.dot_general(a, b, (((1,), (1,)), ((), ())), preferred_element_type=F32)


def iota(shape, dim):
    return lax.broadcasted_iota(jnp.int32, shape, dim)


def layer_kernel(
    n_seq, heads, head_dim,
    tok_hbm, wqkv_hbm, wgate_hbm, cmed_hbm, ccoarse_hbm, gid_hbm, wout_hbm,
    out_hbm,
    tok, halo, wqkv, wgate, wout, cmed, ccoarse, gid, cmed32, ccoarse32,
    kbuf, vnat, vt, q1, q2, gate_t, bias_m, bias_c, medsend, near, csend, crecv, cf32, mkeys, mvt, ckeys, cvt,
    sbuf, pbuf, fbuf, qbuf, fcbuf, qcbuf, acc, mixed, obuf,
    in_sems, out_sems, rim_sems, relay_sems, med_send, med_recv, c_send, c_recv, swap_sems, above,
):
    rows = tok.shape[0]
    inner = heads * head_dim
    pairs = inner // LANES
    per_pair = LANES // head_dim
    med_len = cmed.shape[2]
    coarse_len = ccoarse.shape[2]
    nmed = rows // med_len
    nco = rows // coarse_len
    nblk = gid.shape[1]
    nb = rows // WINDOW
    wide = per_pair * WINDOW
    near_rows = (REACH + 1) * nmed
    scale = head_dim ** (-0.5)
    pos = lax.axis_index("seq")
    rep = lax.axis_index("rep")

    def load(i, src, dst):
        return pltpu.make_async_copy(src, dst, in_sems.at[i])

    loads = [
        load(0, tok_hbm, tok),
        load(1, wqkv_hbm.at[:, inner : 2 * inner], wqkv.at[1]),
        load(2, cmed_hbm, cmed),
        load(3, ccoarse_hbm, ccoarse),
        load(4, wqkv_hbm.at[:, 2 * inner :], wqkv.at[2]),
        load(5, gid_hbm, gid),
        load(6, wqkv_hbm.at[:, :inner], wqkv.at[0]),
        load(7, wgate_hbm, wgate),
        load(8, wout_hbm, wout),
    ]
    for copy in loads:
        copy.start()

    near[...] = jnp.zeros(near.shape, BF16)
    crecv[...] = jnp.zeros(crecv.shape, BF16)
    halo[...] = jnp.zeros(halo.shape, BF16)
    mkeys[...] = jnp.zeros(mkeys.shape, BF16)
    mvt[...] = jnp.zeros(mvt.shape, BF16)

    barrier = pltpu.get_barrier_semaphore()

    def greet(j, carry):
        pl.semaphore_signal(barrier, inc=1, device_id=(rep, j), device_id_type=MESH)
        return carry

    lax.fori_loop(jnp.maximum(pos - NEAR, 0), pos, greet, 0)
    lax.fori_loop(pos + 1, jnp.minimum(pos + NEAR + 1, n_seq), greet, 0)
    odd = lax.rem(pos, 2)
    rounds = (n_seq - 2) // NEAR
    half_seq = n_seq // 2
    chip = pos // 2

    loads[2].wait()
    loads[3].wait()
    cmed32[...] = cmed[...].astype(F32)
    ccoarse32[...] = ccoarse[...].astype(F32)
    spread = jnp.where(iota((med_len, rows), 1) % med_len == iota((med_len, rows), 0), 1.0, 0.0)
    spread = spread.astype(BF16)
    in_med = jnp.where(iota((nmed, rows), 1) // med_len == iota((nmed, rows), 0), 1.0, 0.0)
    in_co = jnp.where(iota((8, rows), 1) // coarse_len == iota((8, rows), 0), 1.0, 0.0)
    group = 2 * per_pair
    groups = heads // group
    glanes = 2 * LANES

    def mixers(kv):
        med_w = dot(cmed32[:, kv, :].astype(BF16), spread)
        co_w = jnp.concatenate([ccoarse32[:, kv, :]] * nco, axis=1)
        out = []
        for g in range(groups):
            hs = range(g * group, (g + 1) * group)
            parts = [med_w[h : h + 1, :] * in_med for h in hs]
            parts += [co_w[h : h + 1, :] * in_co for h in hs]
            out.append(jnp.concatenate(parts, axis=0).astype(BF16))
        return out

    lane_head = iota((1, glanes), 1) // head_dim

    def compressed(mixer, block):
        res = dot(mixer, block)
        med = jnp.zeros((nmed, glanes), F32)
        co = jnp.zeros((8, glanes), F32)
        for i in range(group):
            med = jnp.where(lane_head == i, res[i * nmed : (i + 1) * nmed], med)
            base = group * nmed + 8 * i
            co = jnp.where(lane_head == i, res[base : base + 8], co)
        return med, co

    mix = [mixers(0), mixers(1)]
    co_parts = [[], []]

    def project(kv, g):
        low = dot(tok[...], wqkv[1 + kv, :, g * glanes : (g + 1) * glanes]).astype(BF16)
        for e in range(2):
            cols = slice(e * LANES, (e + 1) * LANES)
            if kv == 0:
                kbuf[2 * g + e, WINDOW:, :] = low[:, cols]
            else:
                vnat[2 * g + e] = low[:, cols]

    def compress(kv, g):
        if kv == 0:
            block = jnp.concatenate([kbuf[2 * g + e, WINDOW:, :] for e in range(2)], axis=1)
        else:
            block = jnp.concatenate([vnat[2 * g + e] for e in range(2)], axis=1)
        med, co = compressed(mix[kv][g], block)
        co_parts[kv].append(co[:nco])
        for e in range(2):
            p = 2 * g + e
            part = med[:, e * LANES : (e + 1) * LANES].astype(BF16)
            medsend[kv * pairs + p] = part
            near[REACH, kv * pairs + p] = part

    def rim_copy():
        return pltpu.make_async_remote_copy(
            src_ref=tok_hbm.at[rows - WINDOW :], dst_ref=halo,
            send_sem=rim_sems.at[0], recv_sem=rim_sems.at[1],
            device_id=(rep, lax.rem(pos + 1, n_seq)), device_id_type=MESH,
        )

    def med_copy(kv, d):
        half = slice(kv * pairs, (kv + 1) * pairs)
        return pltpu.make_async_remote_copy(
            src_ref=medsend.at[half], dst_ref=near.at[REACH - d, half],
            send_sem=med_send.at[kv, d - 1], recv_sem=med_recv.at[kv, d - 1],
            device_id=(rep, lax.rem(pos + d, n_seq)), device_id_type=MESH,
        )

    def coarse_copy(d, slot):
        return pltpu.make_async_remote_copy(
            src_ref=csend, dst_ref=crecv.at[odd * half_seq + slot],
            send_sem=c_send.at[d], recv_sem=c_recv.at[slot],
            device_id=(rep, lax.rem(pos + 2 * d, n_seq)), device_id_type=MESH,
        )

    def swap_copy(side):
        blocks = crecv.at[pl.ds(side * half_seq, half_seq)]
        return pltpu.make_async_remote_copy(
            src_ref=blocks, dst_ref=blocks,
            send_sem=swap_sems.at[0], recv_sem=swap_sems.at[1],
            device_id=(rep, pos + 1 - 2 * odd), device_id_type=MESH,
        )

    def pass_down():
        pl.semaphore_signal(above, inc=1, device_id=(rep, jnp.maximum(pos - NEAR, 0)), device_id_type=MESH)

    def entered():
        pl.semaphore_wait(barrier, jnp.minimum(pos, NEAR) + jnp.minimum(n_seq - 1 - pos, NEAR))

        @pl.when(pos + 1 < n_seq)
        def _():
            rim_copy().start()

        @pl.when(jnp.logical_and(pos >= NEAR, pos + 1 < n_seq))
        def _():
            pass_down()

    def hear(t):
        more = pos + NEAR * t + 1 < n_seq

        @pl.when(more)
        def _():
            pl.semaphore_wait(above, 1)

        @pl.when(jnp.logical_and(more, pos >= NEAR))
        def _():
            pass_down()

    direct = ((1, odd == 0), (2, True), (3, odd == 1))

    def relay_copy(kv, slot):
        half = slice(kv * pairs, (kv + 1) * pairs)
        return pltpu.make_async_remote_copy(
            src_ref=near.at[REACH - 2, half], dst_ref=near.at[slot, half],
            send_sem=relay_sems.at[kv, 0], recv_sem=relay_sems.at[kv, 1],
            device_id=(rep, pos + 1 - 2 * odd), device_id_type=MESH,
        )

    def send_medium(kv):
        for d, sends in direct:
            @pl.when(jnp.logical_and(pos + d < n_seq, sends))
            def _(d=d):
                med_copy(kv, d).start()

    pl.when(pos >= FRONT)(entered)
    loads[0].wait()
    steps = [(kv, g) for kv in range(2) for g in range(groups)]
    for k in range(len(steps) + 1):
        if k < len(steps):
            kv, g = steps[k]
            if g == 0:
                loads[1 if kv == 0 else 4].wait()
            project(kv, g)
        if k > 0:
            compress(*steps[k - 1])
            if steps[k - 1] == (0, groups - 1):
                pl.when(pos < FRONT)(entered)
                send_medium(0)
                pl.when(pos >= NEAR)(functools.partial(hear, 1))
    coarse_rows = [jnp.concatenate(parts, axis=1) for parts in co_parts]
    own_coarse = jnp.concatenate(coarse_rows, axis=0).astype(BF16)
    csend[...] = own_coarse
    crecv[odd * half_seq + chip] = own_coarse

    send_medium(1)

    def send_coarse(d, carry):
        coarse_copy(d, chip).start()
        return carry

    def send_far(t):
        first = NEAR // 2 * t + 1
        lax.fori_loop(first, jnp.minimum(first + NEAR // 2, half_seq - chip), send_coarse, 0)

    def hear_and_send(t, carry):
        hear(t)
        send_far(t)
        return carry

    send_far(0)
    pl.when(pos < NEAR)(functools.partial(hear, 1))
    send_far(1)

    loads[6].wait()
    loads[7].wait()
    loads[5].wait()
    lane = iota((1, LANES), 1) // head_dim
    for g in range(groups):
        full = dot(tok[...], wqkv[0, :, g * glanes : (g + 1) * glanes]) * scale
        for e in range(2):
            part = full[:, e * LANES : (e + 1) * LANES]
            q1[2 * g + e] = part.astype(BF16)
            for h in range(per_pair):
                only = jnp.where(lane == h, part, 0.0).astype(BF16)
                for i in range(nb):
                    q2[2 * g + e, i, h * WINDOW : (h + 1) * WINDOW, :] = only[
                        i * WINDOW : (i + 1) * WINDOW
                    ]
    for p in range(pairs):
        vt[p, :, WINDOW:] = vnat[p].T
    turned = jax.nn.sigmoid(dot_t(wgate[...], tok[...]))
    for level in range(3):
        for h in range(heads):
            row = level * per_pair + h % per_pair
            src = level * heads + h
            gate_t[h // per_pair, row : row + 1, :] = turned[src : src + 1, :]

    hear_and_send(2, 0)
    first_blk = (pos - REACH) * nmed
    key_blk = first_blk + iota((near_rows, nblk), 0)
    gid_row = gid[...].astype(F32)
    key_group = jnp.sum(
        jnp.where(iota((near_rows, nblk), 1) == key_blk, gid_row, 0.0), axis=1, keepdims=True
    )
    own_group = key_group[REACH * nmed :]
    tok_group = jnp.sum(in_med * own_group, axis=0, keepdims=True)
    rel_blk = iota((near_rows, rows), 0)
    seen = (
        (key_group == tok_group)
        & ((rel_blk - REACH * nmed) * med_len + med_len - 1 <= iota((near_rows, rows), 1))
        & (rel_blk + first_blk >= 0)
    )
    bias_m[...] = jnp.where(seen, 0.0, NEG)
    krow = iota((n_seq * nco, rows), 0)
    slot_of = krow % n_seq
    cblk = (2 * (slot_of % half_seq) + slot_of // half_seq) * nco + krow // n_seq
    seen_c = cblk * coarse_len + coarse_len - 1 <= pos * rows + iota((n_seq * nco, rows), 1)
    bias_c[...] = jnp.where(seen_c, 0.0, NEG)

    older = iota((WINDOW, wide), 0) > iota((WINDOW, wide), 1) % WINDOW
    first_bias = jnp.where(pos == 0, NEG, 0.0).astype(F32)

    def gated(res, level, p, i):
        out = []
        for h in range(per_pair):
            src = level * per_pair + h
            row = gate_t[p, src : src + 1, i * WINDOW : (i + 1) * WINDOW]
            out.append(
                res[h * head_dim : (h + 1) * head_dim, h * WINDOW : (h + 1) * WINDOW] * row
            )
        return jnp.concatenate(out, axis=0)

    queue = []

    def enqueue(units, stages, width):
        first = len(queue)
        for b, a in enumerate(range(0, len(units), width)):
            queue.append((stages, units[a : a + width], (first + b) % SLOTS * width))
        return first

    def run_queue(hooks):
        for k in range(len(queue) + SLOTS - 1):
            for hook in hooks.get(k, ()):
                hook()
            for t in range(SLOTS):
                if 0 <= k - t < len(queue):
                    stages, units, base = queue[k - t]
                    if t < len(stages):
                        for j, unit in enumerate(units):
                            stages[t](*unit, base + j)

    def window_scores(p, i, slot):
        keys = kbuf[p, i * WINDOW : (i + 2) * WINDOW, :]
        scores = dot_t(keys, q2[p, i])
        prev = scores[:WINDOW]
        if i == 0:
            prev = prev + first_bias
        sbuf[slot, :WINDOW] = jnp.where(older, prev, scores[WINDOW:])

    def window_soft(p, i, slot):
        for h in range(per_pair):
            cols = slice(h * WINDOW, (h + 1) * WINDOW)
            both = sbuf[slot, :WINDOW, cols]
            terms = jnp.exp(both - jnp.max(both, axis=0, keepdims=True))
            probs = terms * (1.0 / jnp.sum(terms, axis=0, keepdims=True))
            mask = older[:, cols]
            pbuf[slot, :WINDOW, cols] = jnp.where(mask, probs, 0.0).astype(BF16)
            pbuf[slot, WINDOW:, cols] = jnp.where(mask, 0.0, probs).astype(BF16)

    def window_values(p, i, slot):
        res = dot(vt[p, :, i * WINDOW : (i + 2) * WINDOW], pbuf[slot])
        acc[p, :, i * WINDOW : (i + 1) * WINDOW] = gated(res, 0, p, i)

    window_stages = (window_scores, window_soft, window_values)
    inside = [(p, i) for p in range(pairs) for i in range(1, nb)]
    enqueue(inside, window_stages, WINDOW_UNITS)

    def take_rim():
        @pl.when(pos > 0)
        def _():
            rim_copy().wait_recv()

        for kv in range(2):
            for g in range(groups):
                full = dot(halo[...], wqkv[1 + kv, :, g * glanes : (g + 1) * glanes])
                for e in range(2):
                    cols = slice(e * LANES, (e + 1) * LANES)
                    if kv == 0:
                        kbuf[2 * g + e, :WINDOW, :] = full[:, cols].astype(BF16)
                    else:
                        vt[2 * g + e, :, :WINDOW] = full[:, cols].astype(BF16).T

    def send_rest():
        lax.fori_loop(3, rounds + 1, hear_and_send, 0)


    def relay(kv):
        @pl.when(pos >= 2)
        def _():
            med_copy(kv, 2).wait_recv()
            relay_copy(kv, odd * (REACH - 1)).start()

    at_first = enqueue([(p, 0) for p in range(pairs)], window_stages, WINDOW_UNITS)

    def take_medium(kv):
        for d, sender in ((1, odd == 1), (3, odd == 0)):
            @pl.when(jnp.logical_and(pos >= d, sender))
            def _(d=d):
                med_copy(kv, d).wait_recv()

        @pl.when(pos >= 2)
        def _():
            relay_copy(kv, (1 - odd) * (REACH - 1)).wait_recv()

    def lay_keys():
        take_medium(0)
        for p in range(pairs):
            for h in range(per_pair):
                lanes = slice(h * head_dim, (h + 1) * head_dim)
                for r in range(REACH + 1):
                    base = h * near_rows + r * nmed
                    mkeys[p, base : base + nmed, lanes] = near[r, p, :, lanes]

    def lay_values():
        take_medium(1)
        for p in range(pairs):
            values = jnp.concatenate([near[r, pairs + p] for r in range(REACH + 1)], axis=0)
            turned = values.T
            for h in range(per_pair):
                lanes = slice(h * head_dim, (h + 1) * head_dim)
                mvt[p, lanes, h * near_rows : (h + 1) * near_rows] = turned[lanes, :]

    ncoarse = n_seq * nco
    nf = rows // FAR

    def mix_gate(res, level, p, cols):
        out = []
        for h in range(per_pair):
            row = gate_t[p, level * per_pair + h : level * per_pair + h + 1, cols]
            out.append(res[h * head_dim : (h + 1) * head_dim] * row)
        return jnp.concatenate(out, axis=0)

    def sink_soft(src, dst, slot, count):
        for h in range(per_pair):
            part = slice(h * count, (h + 1) * count)
            scores = src[slot, part]
            peak = jnp.maximum(jnp.max(scores, axis=0, keepdims=True), 0.0)
            terms = jnp.exp(scores - peak)
            total = jnp.exp(-peak) + jnp.sum(terms, axis=0, keepdims=True)
            dst[slot, part] = (terms * (1.0 / total)).astype(BF16)

    def medium_scores(p, i, slot):
        cols = slice(i * FAR, (i + 1) * FAR)
        scores = dot_t(mkeys[p], q1[p, cols, :])
        for h in range(per_pair):
            part = slice(h * near_rows, (h + 1) * near_rows)
            fbuf[slot, part] = scores[part] + bias_m[:, cols]

    def medium_soft(p, i, slot):
        sink_soft(fbuf, qbuf, slot, near_rows)

    def medium_values(p, i, slot):
        cols = slice(i * FAR, (i + 1) * FAR)
        acc[p, :, cols] += mix_gate(dot(mvt[p], qbuf[slot]), 1, p, cols)

    far_units = [(p, i) for p in range(pairs) for i in range(nf)]
    at_medium = enqueue(far_units, (medium_scores, medium_soft, medium_values), MEDIUM_UNITS)

    def take_coarse(j, carry):
        coarse_copy(1, j).wait_recv()
        return carry

    def widen(j, carry):
        cf32[j] = crecv[j].astype(F32)
        return carry

    def swap_coarse():
        lax.fori_loop(0, chip, take_coarse, 0)
        swap_copy(odd).start()

    def lay_coarse():
        swap_copy(1 - odd).wait_recv()
        lax.fori_loop(0, n_seq, widen, 0)
        for p in range(pairs):
            cols = slice(p * LANES, (p + 1) * LANES)
            ck = jnp.concatenate([cf32[:, j, cols] for j in range(nco)], axis=0)
            cv = jnp.concatenate([cf32[:, nco + j, cols] for j in range(nco)], axis=0)
            ckeys[p] = jnp.concatenate([jnp.where(lane == h, ck, 0.0) for h in range(per_pair)], axis=0).astype(BF16)
            cv = jnp.concatenate([jnp.where(lane == h, cv, 0.0) for h in range(per_pair)], axis=0)
            cvt[p] = cv.T.astype(BF16)

    def store_rows(i):
        part = slice(i * FAR, (i + 1) * FAR)
        return pltpu.make_async_copy(obuf.at[part], out_hbm.at[part], out_sems.at[i])

    def coarse_scores(p, i, slot):
        cols = slice(i * FAR, (i + 1) * FAR)
        scores = dot_t(ckeys[p], q1[p, cols, :])
        for h in range(per_pair):
            part = slice(h * ncoarse, (h + 1) * ncoarse)
            fcbuf[slot, part] = scores[part] + bias_c[:, cols]

    def coarse_soft(p, i, slot):
        sink_soft(fcbuf, qcbuf, slot, ncoarse)

    def coarse_values(p, i, slot):
        cols = slice(i * FAR, (i + 1) * FAR)
        total = acc[p, :, cols] + mix_gate(dot(cvt[p], qcbuf[slot]), 2, p, cols)
        mixed[cols, p * LANES : (p + 1) * LANES] = total.astype(BF16).T

    def project_out(p, i, slot):
        if p == pairs - 1:
            part = slice(i * FAR, (i + 1) * FAR)
            obuf[part] = dot(mixed[part], wout[...]).astype(BF16)
            store_rows(i).start()

    by_rows = [(p, i) for i in range(nf) for p in range(pairs)]
    at_coarse = enqueue(by_rows, (coarse_scores, coarse_soft, coarse_values, project_out), COARSE_UNITS)
    run_queue({
        at_first: (take_rim,),
        at_first + 1: (functools.partial(relay, 0), send_rest),
        at_first + 2: (functools.partial(relay, 1),),
        at_medium: (lay_keys,),
        at_medium + 2: (lay_values,),
        at_medium + 3: (swap_coarse,),
        at_coarse: (loads[8].wait, lay_coarse),
    })

    @pl.when(pos + 1 < n_seq)
    def _():
        rim_copy().wait_send()

    @pl.when(pos >= 2)
    def _():
        relay_copy(0, odd * (REACH - 1)).wait_send()
        relay_copy(1, odd * (REACH - 1)).wait_send()

    for d, sends in direct:
        @pl.when(jnp.logical_and(pos + d < n_seq, sends))
        def _(d=d):
            med_copy(0, d).wait_send()
            med_copy(1, d).wait_send()

    def sent_coarse(k, carry):
        coarse_copy(k, chip).wait_send()
        return carry

    lax.fori_loop(1, half_seq - chip, sent_coarse, 0)
    swap_copy(odd).wait_send()
    for i in range(nf):
        store_rows(i).wait()


def shards(tokens, w_qkv, w_gate, w_out, cmp_med, cmp_coarse, group_id):
    n_seq = lax.axis_size("seq")
    rows, width = tokens.shape
    heads = cmp_med.shape[1]
    inner = w_out.shape[0]
    head_dim = inner // heads
    med_len, coarse_len = cmp_med.shape[2], cmp_coarse.shape[2]
    nmed, nco = rows // med_len, rows // coarse_len
    pairs = inner // LANES
    per_pair = LANES // head_dim
    nb = rows // WINDOW
    gid = group_id.reshape(1, -1)
    cmed, ccoarse = jnp.swapaxes(cmp_med, 0, 1), jnp.swapaxes(cmp_coarse, 0, 1)
    med_keys = per_pair * (REACH + 1) * nmed
    coarse_keys = per_pair * n_seq * nco
    operands = (tokens, w_qkv, w_gate.T, cmed, ccoarse, gid, w_out)
    anywhere = pl.BlockSpec(memory_space=pl.ANY)
    vmem = pltpu.VMEM
    sem = pltpu.SemaphoreType.DMA
    return pl.pallas_call(
        functools.partial(layer_kernel, n_seq, heads, head_dim),
        out_shape=jax.ShapeDtypeStruct((rows, w_out.shape[1]), BF16),
        in_specs=[pl.BlockSpec(memory_space=pltpu.HBM)] * 7,
        out_specs=anywhere,
        scratch_shapes=[
            vmem((rows, width), BF16),
            vmem((WINDOW, width), BF16),
            vmem((3, width, inner), BF16),
            vmem(w_gate.shape[::-1], BF16),
            vmem(w_out.shape, BF16),
            vmem(cmed.shape, BF16),
            vmem(ccoarse.shape, BF16),
            vmem(gid.shape, jnp.int32),
            vmem(cmed.shape, F32),
            vmem(ccoarse.shape, F32),
            vmem((pairs, WINDOW + rows, LANES), BF16),
            vmem((pairs, rows, LANES), BF16),
            vmem((pairs, LANES, WINDOW + rows), BF16),
            vmem((pairs, rows, LANES), BF16),
            vmem((pairs, nb, per_pair * WINDOW, LANES), BF16),
            vmem((pairs, 8, rows), F32),
            vmem(((REACH + 1) * nmed, rows), F32),
            vmem((n_seq * nco, rows), F32),
            vmem((2 * pairs, nmed, LANES), BF16),
            vmem((REACH + 1, 2 * pairs, nmed, LANES), BF16),
            vmem((2 * nco, inner), BF16),
            vmem((n_seq, 2 * nco, inner), BF16),
            vmem((n_seq, 2 * nco, inner), F32),
            vmem((pairs, med_keys, LANES), BF16),
            vmem((pairs, LANES, med_keys), BF16),
            vmem((pairs, coarse_keys, LANES), BF16),
            vmem((pairs, LANES, coarse_keys), BF16),
            vmem((SLOTS * WINDOW_UNITS, WINDOW, per_pair * WINDOW), F32),
            vmem((SLOTS * WINDOW_UNITS, 2 * WINDOW, per_pair * WINDOW), BF16),
            vmem((SLOTS * MEDIUM_UNITS, med_keys, FAR), F32),
            vmem((SLOTS * MEDIUM_UNITS, med_keys, FAR), BF16),
            vmem((SLOTS * COARSE_UNITS, coarse_keys, FAR), F32),
            vmem((SLOTS * COARSE_UNITS, coarse_keys, FAR), BF16),
            vmem((pairs, LANES, rows), F32),
            vmem((rows, inner), BF16),
            vmem((rows, w_out.shape[1]), BF16),
            sem((9,)),
            sem((rows // FAR,)),
            sem((2,)),
            sem((2, 2)),
            sem((2, REACH)),
            sem((2, REACH)),
            sem((n_seq // 2,)),
            sem((n_seq // 2,)),
            sem((2,)),
            pltpu.SemaphoreType.REGULAR,
        ],
        compiler_params=pltpu.CompilerParams(
            collective_id=0, has_side_effects=True, vmem_limit_bytes=48 * 1024 * 1024
        ),
        name="sparse_layer",
    )(*[pltpu.with_memory_space_constraint(x, pltpu.HBM) for x in operands])


def solution(mesh):
    placed = (P(("rep", "seq"), None), P(), P(), P(), P(), P(), P("rep"))
    return jax.shard_map(
        shards, mesh=mesh, in_specs=placed, out_specs=P(("rep", "seq"), None), check_vma=False
    )
```

```python
import functools
import jax
import jax.numpy as jnp
from jax import lax
from jax.experimental import pallas as pl
from jax.experimental.pallas import tpu as pltpu
from jax.sharding import PartitionSpec as P

WINDOW = 128
REACH = 3
SLOTS = 4
WINDOW_UNITS = 2
MEDIUM_UNITS = 2
COARSE_UNITS = 6
LANES = 128
NEAR = 4
FAR = 256
FRONT = 2
NEG = -1e30
F32 = jnp.float32
BF16 = jnp.bfloat16
MESH = pl.DeviceIdType.MESH


def dot(a, b):
    return jnp.dot(a, b, preferred_element_type=F32)


def dot_t(a, b):
    return lax.dot_general(a, b, (((1,), (1,)), ((), ())), preferred_element_type=F32)


def iota(shape, dim):
    return lax.broadcasted_iota(jnp.int32, shape, dim)


def layer_kernel(
    n_seq, heads, head_dim,
    tok_hbm, wqkv_hbm, wgate_hbm, cmed_hbm, ccoarse_hbm, gid_hbm, wout_hbm,
    out_hbm,
    tok, halo, wqkv, wgate, wout, cmed, ccoarse, gid, cmed32, ccoarse32,
    kbuf, vnat, vt, q1, q2, gate_t, bias_m, bias_c, medsend, near, csend, crecv, cf32, mkeys, mvt, ckeys, cvt,
    sbuf, pbuf, fbuf, qbuf, fcbuf, qcbuf, acc, mixed, obuf,
    in_sems, out_sems, rim_sems, relay_sems, med_send, med_recv, c_send, c_recv, swap_sems, above,
):
    rows = tok.shape[0]
    inner = heads * head_dim
    pairs = inner // LANES
    per_pair = LANES // head_dim
    med_len = cmed.shape[2]
    coarse_len = ccoarse.shape[2]
    nmed = rows // med_len
    nco = rows // coarse_len
    nblk = gid.shape[1]
    nb = rows // WINDOW
    wide = per_pair * WINDOW
    near_rows = (REACH + 1) * nmed
    scale = head_dim ** (-0.5)
    pos = lax.axis_index("seq")
    rep = lax.axis_index("rep")

    def load(i, src, dst):
        return pltpu.make_async_copy(src, dst, in_sems.at[i])

    loads = [
        load(0, tok_hbm, tok),
        load(1, wqkv_hbm.at[:, inner : 2 * inner], wqkv.at[1]),
        load(2, cmed_hbm, cmed),
        load(3, ccoarse_hbm, ccoarse),
        load(4, wqkv_hbm.at[:, 2 * inner :], wqkv.at[2]),
        load(5, gid_hbm, gid),
        load(6, wqkv_hbm.at[:, :inner], wqkv.at[0]),
        load(7, wgate_hbm, wgate),
        load(8, wout_hbm, wout),
    ]
    for copy in loads:
        copy.start()

    near[...] = jnp.zeros(near.shape, BF16)
    crecv[...] = jnp.zeros(crecv.shape, BF16)
    halo[...] = jnp.zeros(halo.shape, BF16)
    mkeys[...] = jnp.zeros(mkeys.shape, BF16)
    mvt[...] = jnp.zeros(mvt.shape, BF16)

    barrier = pltpu.get_barrier_semaphore()

    def greet(j, carry):
        pl.semaphore_signal(barrier, inc=1, device_id=(rep, j), device_id_type=MESH)
        return carry

    lax.fori_loop(jnp.maximum(pos - NEAR, 0), pos, greet, 0)
    lax.fori_loop(pos + 1, jnp.minimum(pos + NEAR + 1, n_seq), greet, 0)
    odd = lax.rem(pos, 2)
    rounds = (n_seq - 2) // NEAR
    half_seq = n_seq // 2
    chip = pos // 2

    loads[2].wait()
    loads[3].wait()
    cmed32[...] = cmed[...].astype(F32)
    ccoarse32[...] = ccoarse[...].astype(F32)
    spread = jnp.where(iota((med_len, rows), 1) % med_len == iota((med_len, rows), 0), 1.0, 0.0)
    spread = spread.astype(BF16)
    in_med = jnp.where(iota((nmed, rows), 1) // med_len == iota((nmed, rows), 0), 1.0, 0.0)
    in_co = jnp.where(iota((8, rows), 1) // coarse_len == iota((8, rows), 0), 1.0, 0.0)
    group = 2 * per_pair
    groups = heads // group
    glanes = 2 * LANES

    def mixers(kv):
        med_w = dot(cmed32[:, kv, :].astype(BF16), spread)
        co_w = jnp.concatenate([ccoarse32[:, kv, :]] * nco, axis=1)
        out = []
        for g in range(groups):
            hs = range(g * group, (g + 1) * group)
            parts = [med_w[h : h + 1, :] * in_med for h in hs]
            parts += [co_w[h : h + 1, :] * in_co for h in hs]
            out.append(jnp.concatenate(parts, axis=0).astype(BF16))
        return out

    lane_head = iota((1, glanes), 1) // head_dim

    def compressed(mixer, block):
        res = dot(mixer, block)
        med = jnp.zeros((nmed, glanes), F32)
        co = jnp.zeros((8, glanes), F32)
        for i in range(group):
            med = jnp.where(lane_head == i, res[i * nmed : (i + 1) * nmed], med)
            base = group * nmed + 8 * i
            co = jnp.where(lane_head == i, res[base : base + 8], co)
        return med, co

    mix = [mixers(0), mixers(1)]
    co_parts = [[], []]

    def project(kv, g):
        low = dot(tok[...], wqkv[1 + kv, :, g * glanes : (g + 1) * glanes]).astype(BF16)
        for e in range(2):
            cols = slice(e * LANES, (e + 1) * LANES)
            if kv == 0:
                kbuf[2 * g + e, WINDOW:, :] = low[:, cols]
            else:
                vnat[2 * g + e] = low[:, cols]

    def compress(kv, g):
        if kv == 0:
            block = jnp.concatenate([kbuf[2 * g + e, WINDOW:, :] for e in range(2)], axis=1)
        else:
            block = jnp.concatenate([vnat[2 * g + e] for e in range(2)], axis=1)
        med, co = compressed(mix[kv][g], block)
        co_parts[kv].append(co[:nco])
        for e in range(2):
            p = 2 * g + e
            part = med[:, e * LANES : (e + 1) * LANES].astype(BF16)
            medsend[kv * pairs + p] = part
            near[REACH, kv * pairs + p] = part

    def rim_copy():
        return pltpu.make_async_remote_copy(
            src_ref=tok_hbm.at[rows - WINDOW :], dst_ref=halo,
            send_sem=rim_sems.at[0], recv_sem=rim_sems.at[1],
            device_id=(rep, lax.rem(pos + 1, n_seq)), device_id_type=MESH,
        )

    def med_copy(kv, d):
        half = slice(kv * pairs, (kv + 1) * pairs)
        return pltpu.make_async_remote_copy(
            src_ref=medsend.at[half], dst_ref=near.at[REACH - d, half],
            send_sem=med_send.at[kv, d - 1], recv_sem=med_recv.at[kv, d - 1],
            device_id=(rep, lax.rem(pos + d, n_seq)), device_id_type=MESH,
        )

    def coarse_copy(d, slot):
        return pltpu.make_async_remote_copy(
            src_ref=csend, dst_ref=crecv.at[odd * half_seq + slot],
            send_sem=c_send.at[d], recv_sem=c_recv.at[slot],
            device_id=(rep, lax.rem(pos + 2 * d, n_seq)), device_id_type=MESH,
        )

    def swap_copy(side):
        blocks = crecv.at[pl.ds(side * half_seq, half_seq)]
        return pltpu.make_async_remote_copy(
            src_ref=blocks, dst_ref=blocks,
            send_sem=swap_sems.at[0], recv_sem=swap_sems.at[1],
            device_id=(rep, pos + 1 - 2 * odd), device_id_type=MESH,
        )

    def pass_down():
        pl.semaphore_signal(above, inc=1, device_id=(rep, jnp.maximum(pos - NEAR, 0)), device_id_type=MESH)

    def entered():
        pl.semaphore_wait(barrier, jnp.minimum(pos, NEAR) + jnp.minimum(n_seq - 1 - pos, NEAR))

        @pl.when(pos + 1 < n_seq)
        def _():
            rim_copy().start()

        @pl.when(jnp.logical_and(pos >= NEAR, pos + 1 < n_seq))
        def _():
            pass_down()

    def hear(t):
        more = pos + NEAR * t + 1 < n_seq

        @pl.when(more)
        def _():
            pl.semaphore_wait(above, 1)

        @pl.when(jnp.logical_and(more, pos >= NEAR))
        def _():
            pass_down()

    direct = ((1, odd == 0), (2, True), (3, odd == 1))

    def relay_copy(kv, slot):
        half = slice(kv * pairs, (kv + 1) * pairs)
        return pltpu.make_async_remote_copy(
            src_ref=near.at[REACH - 2, half], dst_ref=near.at[slot, half],
            send_sem=relay_sems.at[kv, 0], recv_sem=relay_sems.at[kv, 1],
            device_id=(rep, pos + 1 - 2 * odd), device_id_type=MESH,
        )

    def send_medium(kv):
        for d, sends in direct:
            @pl.when(jnp.logical_and(pos + d < n_seq, sends))
            def _(d=d):
                med_copy(kv, d).start()

    pl.when(pos >= FRONT)(entered)
    loads[0].wait()
    steps = [(kv, g) for kv in range(2) for g in range(groups)]
    for k in range(len(steps) + 1):
        if k < len(steps):
            kv, g = steps[k]
            if g == 0:
                loads[1 if kv == 0 else 4].wait()
            project(kv, g)
        if k > 0:
            compress(*steps[k - 1])
            if steps[k - 1] == (0, groups - 1):
                pl.when(pos < FRONT)(entered)
                send_medium(0)
                pl.when(pos >= NEAR)(functools.partial(hear, 1))
    coarse_rows = [jnp.concatenate(parts, axis=1) for parts in co_parts]
    own_coarse = jnp.concatenate(coarse_rows, axis=0).astype(BF16)
    csend[...] = own_coarse
    crecv[odd * half_seq + chip] = own_coarse

    send_medium(1)

    def send_coarse(d, carry):
        coarse_copy(d, chip).start()
        return carry

    def send_far(t):
        first = NEAR // 2 * t + 1
        lax.fori_loop(first, jnp.minimum(first + NEAR // 2, half_seq - chip), send_coarse, 0)

    def hear_and_send(t, carry):
        hear(t)
        send_far(t)
        return carry

    send_far(0)
    pl.when(pos < NEAR)(functools.partial(hear, 1))
    send_far(1)

    loads[6].wait()
    loads[7].wait()
    loads[5].wait()
    lane = iota((1, LANES), 1) // head_dim
    for g in range(groups):
        full = dot(tok[...], wqkv[0, :, g * glanes : (g + 1) * glanes]) * scale
        for e in range(2):
            part = full[:, e * LANES : (e + 1) * LANES]
            q1[2 * g + e] = part.astype(BF16)
            for h in range(per_pair):
                only = jnp.where(lane == h, part, 0.0).astype(BF16)
                for i in range(nb):
                    q2[2 * g + e, i, h * WINDOW : (h + 1) * WINDOW, :] = only[
                        i * WINDOW : (i + 1) * WINDOW
                    ]
    for p in range(pairs):
        vt[p, :, WINDOW:] = vnat[p].T
    turned = jax.nn.sigmoid(dot_t(wgate[...], tok[...]))
    for level in range(3):
        for h in range(heads):
            row = level * per_pair + h % per_pair
            src = level * heads + h
            gate_t[h // per_pair, row : row + 1, :] = turned[src : src + 1, :]

    hear_and_send(2, 0)
    first_blk = (pos - REACH) * nmed
    key_blk = first_blk + iota((near_rows, nblk), 0)
    gid_row = gid[...].astype(F32)
    key_group = jnp.sum(
        jnp.where(iota((near_rows, nblk), 1) == key_blk, gid_row, 0.0), axis=1, keepdims=True
    )
    own_group = key_group[REACH * nmed :]
    tok_group = jnp.sum(in_med * own_group, axis=0, keepdims=True)
    rel_blk = iota((near_rows, rows), 0)
    seen = (
        (key_group == tok_group)
        & ((rel_blk - REACH * nmed) * med_len + med_len - 1 <= iota((near_rows, rows), 1))
        & (rel_blk + first_blk >= 0)
    )
    bias_m[...] = jnp.where(seen, 0.0, NEG)
    krow = iota((n_seq * nco, rows), 0)
    slot_of = krow % n_seq
    cblk = (2 * (slot_of % half_seq) + slot_of // half_seq) * nco + krow // n_seq
    seen_c = cblk * coarse_len + coarse_len - 1 <= pos * rows + iota((n_seq * nco, rows), 1)
    bias_c[...] = jnp.where(seen_c, 0.0, NEG)

    older = iota((WINDOW, wide), 0) > iota((WINDOW, wide), 1) % WINDOW
    first_bias = jnp.where(pos == 0, NEG, 0.0).astype(F32)

    def gated(res, level, p, i):
        out = []
        for h in range(per_pair):
            src = level * per_pair + h
            row = gate_t[p, src : src + 1, i * WINDOW : (i + 1) * WINDOW]
            out.append(
                res[h * head_dim : (h + 1) * head_dim, h * WINDOW : (h + 1) * WINDOW] * row
            )
        return jnp.concatenate(out, axis=0)

    queue = []

    def enqueue(units, stages, width):
        first = len(queue)
        for b, a in enumerate(range(0, len(units), width)):
            queue.append((stages, units[a : a + width], (first + b) % SLOTS * width))
        return first

    def run_queue(hooks):
        for k in range(len(queue) + SLOTS - 1):
            for hook in hooks.get(k, ()):
                hook()
            for t in range(SLOTS):
                if 0 <= k - t < len(queue):
                    stages, units, base = queue[k - t]
                    if t < len(stages):
                        for j, unit in enumerate(units):
                            stages[t](*unit, base + j)

    def window_scores(p, i, slot):
        keys = kbuf[p, i * WINDOW : (i + 2) * WINDOW, :]
        scores = dot_t(keys, q2[p, i])
        prev = scores[:WINDOW]
        if i == 0:
            prev = prev + first_bias
        sbuf[slot, :WINDOW] = jnp.where(older, prev, scores[WINDOW:])

    def window_soft(p, i, slot):
        for h in range(per_pair):
            cols = slice(h * WINDOW, (h + 1) * WINDOW)
            both = sbuf[slot, :WINDOW, cols]
            terms = jnp.exp(both - jnp.max(both, axis=0, keepdims=True))
            probs = terms * (1.0 / jnp.sum(terms, axis=0, keepdims=True))
            mask = older[:, cols]
            pbuf[slot, :WINDOW, cols] = jnp.where(mask, probs, 0.0).astype(BF16)
            pbuf[slot, WINDOW:, cols] = jnp.where(mask, 0.0, probs).astype(BF16)

    def window_values(p, i, slot):
        res = dot(vt[p, :, i * WINDOW : (i + 2) * WINDOW], pbuf[slot])
        acc[p, :, i * WINDOW : (i + 1) * WINDOW] = gated(res, 0, p, i)

    window_stages = (window_scores, window_soft, window_values)
    inside = [(p, i) for p in range(pairs) for i in range(1, nb)]
    enqueue(inside, window_stages, WINDOW_UNITS)

    def take_rim():
        @pl.when(pos > 0)
        def _():
            rim_copy().wait_recv()

        for kv in range(2):
            for g in range(groups):
                full = dot(halo[...], wqkv[1 + kv, :, g * glanes : (g + 1) * glanes])
                for e in range(2):
                    cols = slice(e * LANES, (e + 1) * LANES)
                    if kv == 0:
                        kbuf[2 * g + e, :WINDOW, :] = full[:, cols].astype(BF16)
                    else:
                        vt[2 * g + e, :, :WINDOW] = full[:, cols].astype(BF16).T

    def send_rest():
        lax.fori_loop(3, rounds + 1, hear_and_send, 0)


    def relay(kv):
        @pl.when(pos >= 2)
        def _():
            med_copy(kv, 2).wait_recv()
            relay_copy(kv, odd * (REACH - 1)).start()

    at_first = enqueue([(p, 0) for p in range(pairs)], window_stages, WINDOW_UNITS)

    def take_medium(kv):
        for d, sender in ((1, odd == 1), (3, odd == 0)):
            @pl.when(jnp.logical_and(pos >= d, sender))
            def _(d=d):
                med_copy(kv, d).wait_recv()

        @pl.when(pos >= 2)
        def _():
            relay_copy(kv, (1 - odd) * (REACH - 1)).wait_recv()

    def lay_keys():
        take_medium(0)
        for p in range(pairs):
            for h in range(per_pair):
                lanes = slice(h * head_dim, (h + 1) * head_dim)
                for r in range(REACH + 1):
                    base = h * near_rows + r * nmed
                    mkeys[p, base : base + nmed, lanes] = near[r, p, :, lanes]

    def lay_values():
        take_medium(1)
        for p in range(pairs):
            values = jnp.concatenate([near[r, pairs + p] for r in range(REACH + 1)], axis=0)
            turned = values.T
            for h in range(per_pair):
                lanes = slice(h * head_dim, (h + 1) * head_dim)
                mvt[p, lanes, h * near_rows : (h + 1) * near_rows] = turned[lanes, :]

    ncoarse = n_seq * nco
    nf = rows // FAR

    def mix_gate(res, level, p, cols):
        out = []
        for h in range(per_pair):
            row = gate_t[p, level * per_pair + h : level * per_pair + h + 1, cols]
            out.append(res[h * head_dim : (h + 1) * head_dim] * row)
        return jnp.concatenate(out, axis=0)

    def sink_soft(src, dst, slot, count):
        for h in range(per_pair):
            part = slice(h * count, (h + 1) * count)
            scores = src[slot, part]
            peak = jnp.maximum(jnp.max(scores, axis=0, keepdims=True), 0.0)
            terms = jnp.exp(scores - peak)
            total = jnp.exp(-peak) + jnp.sum(terms, axis=0, keepdims=True)
            dst[slot, part] = (terms * (1.0 / total)).astype(BF16)

    def medium_scores(p, i, slot):
        cols = slice(i * FAR, (i + 1) * FAR)
        scores = dot_t(mkeys[p], q1[p, cols, :])
        for h in range(per_pair):
            part = slice(h * near_rows, (h + 1) * near_rows)
            fbuf[slot, part] = scores[part] + bias_m[:, cols]

    def medium_soft(p, i, slot):
        sink_soft(fbuf, qbuf, slot, near_rows)

    def medium_values(p, i, slot):
        cols = slice(i * FAR, (i + 1) * FAR)
        acc[p, :, cols] += mix_gate(dot(mvt[p], qbuf[slot]), 1, p, cols)

    far_units = [(p, i) for p in range(pairs) for i in range(nf)]
    at_medium = enqueue(far_units, (medium_scores, medium_soft, medium_values), MEDIUM_UNITS)

    def take_coarse(j, carry):
        coarse_copy(1, j).wait_recv()
        return carry

    def widen(j, carry):
        cf32[j] = crecv[j].astype(F32)
        return carry

    def swap_coarse():
        lax.fori_loop(0, chip, take_coarse, 0)
        swap_copy(odd).start()

    def lay_coarse():
        swap_copy(1 - odd).wait_recv()
        lax.fori_loop(0, n_seq, widen, 0)
        for p in range(pairs):
            cols = slice(p * LANES, (p + 1) * LANES)
            ck = jnp.concatenate([cf32[:, j, cols] for j in range(nco)], axis=0)
            cv = jnp.concatenate([cf32[:, nco + j, cols] for j in range(nco)], axis=0)
            ckeys[p] = jnp.concatenate([jnp.where(lane == h, ck, 0.0) for h in range(per_pair)], axis=0).astype(BF16)
            cv = jnp.concatenate([jnp.where(lane == h, cv, 0.0) for h in range(per_pair)], axis=0)
            cvt[p] = cv.T.astype(BF16)

    def store_rows(i):
        part = slice(i * FAR, (i + 1) * FAR)
        return pltpu.make_async_copy(obuf.at[part], out_hbm.at[part], out_sems.at[i])

    def coarse_scores(p, i, slot):
        cols = slice(i * FAR, (i + 1) * FAR)
        scores = dot_t(ckeys[p], q1[p, cols, :])
        for h in range(per_pair):
            part = slice(h * ncoarse, (h + 1) * ncoarse)
            fcbuf[slot, part] = scores[part] + bias_c[:, cols]

    def coarse_soft(p, i, slot):
        sink_soft(fcbuf, qcbuf, slot, ncoarse)

    def coarse_values(p, i, slot):
        cols = slice(i * FAR, (i + 1) * FAR)
        total = acc[p, :, cols] + mix_gate(dot(cvt[p], qcbuf[slot]), 2, p, cols)
        mixed[cols, p * LANES : (p + 1) * LANES] = total.astype(BF16).T

    def project_out(p, i, slot):
        if p == pairs - 1:
            part = slice(i * FAR, (i + 1) * FAR)
            obuf[part] = dot(mixed[part], wout[...]).astype(BF16)
            store_rows(i).start()

    by_rows = [(p, i) for i in range(nf) for p in range(pairs)]
    at_coarse = enqueue(by_rows, (coarse_scores, coarse_soft, coarse_values, project_out), COARSE_UNITS)
    run_queue({
        at_first: (take_rim, functools.partial(relay, 0)),
        at_first + 1: (send_rest,),
        at_first + 2: (functools.partial(relay, 1),),
        at_medium: (lay_keys,),
        at_medium + 2: (lay_values,),
        at_medium + 3: (swap_coarse,),
        at_coarse: (loads[8].wait, lay_coarse),
    })

    @pl.when(pos + 1 < n_seq)
    def _():
        rim_copy().wait_send()

    @pl.when(pos >= 2)
    def _():
        relay_copy(0, odd * (REACH - 1)).wait_send()
        relay_copy(1, odd * (REACH - 1)).wait_send()

    for d, sends in direct:
        @pl.when(jnp.logical_and(pos + d < n_seq, sends))
        def _(d=d):
            med_copy(0, d).wait_send()
            med_copy(1, d).wait_send()

    def sent_coarse(k, carry):
        coarse_copy(k, chip).wait_send()
        return carry

    lax.fori_loop(1, half_seq - chip, sent_coarse, 0)
    swap_copy(odd).wait_send()
    for i in range(nf):
        store_rows(i).wait()


def shards(tokens, w_qkv, w_gate, w_out, cmp_med, cmp_coarse, group_id):
    n_seq = lax.axis_size("seq")
    rows, width = tokens.shape
    heads = cmp_med.shape[1]
    inner = w_out.shape[0]
    head_dim = inner // heads
    med_len, coarse_len = cmp_med.shape[2], cmp_coarse.shape[2]
    nmed, nco = rows // med_len, rows // coarse_len
    pairs = inner // LANES
    per_pair = LANES // head_dim
    nb = rows // WINDOW
    gid = group_id.reshape(1, -1)
    cmed, ccoarse = jnp.swapaxes(cmp_med, 0, 1), jnp.swapaxes(cmp_coarse, 0, 1)
    med_keys = per_pair * (REACH + 1) * nmed
    coarse_keys = per_pair * n_seq * nco
    operands = (tokens, w_qkv, w_gate.T, cmed, ccoarse, gid, w_out)
    anywhere = pl.BlockSpec(memory_space=pl.ANY)
    vmem = pltpu.VMEM
    sem = pltpu.SemaphoreType.DMA
    return pl.pallas_call(
        functools.partial(layer_kernel, n_seq, heads, head_dim),
        out_shape=jax.ShapeDtypeStruct((rows, w_out.shape[1]), BF16),
        in_specs=[pl.BlockSpec(memory_space=pltpu.HBM)] * 7,
        out_specs=anywhere,
        scratch_shapes=[
            vmem((rows, width), BF16),
            vmem((WINDOW, width), BF16),
            vmem((3, width, inner), BF16),
            vmem(w_gate.shape[::-1], BF16),
            vmem(w_out.shape, BF16),
            vmem(cmed.shape, BF16),
            vmem(ccoarse.shape, BF16),
            vmem(gid.shape, jnp.int32),
            vmem(cmed.shape, F32),
            vmem(ccoarse.shape, F32),
            vmem((pairs, WINDOW + rows, LANES), BF16),
            vmem((pairs, rows, LANES), BF16),
            vmem((pairs, LANES, WINDOW + rows), BF16),
            vmem((pairs, rows, LANES), BF16),
            vmem((pairs, nb, per_pair * WINDOW, LANES), BF16),
            vmem((pairs, 8, rows), F32),
            vmem(((REACH + 1) * nmed, rows), F32),
            vmem((n_seq * nco, rows), F32),
            vmem((2 * pairs, nmed, LANES), BF16),
            vmem((REACH + 1, 2 * pairs, nmed, LANES), BF16),
            vmem((2 * nco, inner), BF16),
            vmem((n_seq, 2 * nco, inner), BF16),
            vmem((n_seq, 2 * nco, inner), F32),
            vmem((pairs, med_keys, LANES), BF16),
            vmem((pairs, LANES, med_keys), BF16),
            vmem((pairs, coarse_keys, LANES), BF16),
            vmem((pairs, LANES, coarse_keys), BF16),
            vmem((SLOTS * WINDOW_UNITS, WINDOW, per_pair * WINDOW), F32),
            vmem((SLOTS * WINDOW_UNITS, 2 * WINDOW, per_pair * WINDOW), BF16),
            vmem((SLOTS * MEDIUM_UNITS, med_keys, FAR), F32),
            vmem((SLOTS * MEDIUM_UNITS, med_keys, FAR), BF16),
            vmem((SLOTS * COARSE_UNITS, coarse_keys, FAR), F32),
            vmem((SLOTS * COARSE_UNITS, coarse_keys, FAR), BF16),
            vmem((pairs, LANES, rows), F32),
            vmem((rows, inner), BF16),
            vmem((rows, w_out.shape[1]), BF16),
            sem((9,)),
            sem((rows // FAR,)),
            sem((2,)),
            sem((2, 2)),
            sem((2, REACH)),
            sem((2, REACH)),
            sem((n_seq // 2,)),
            sem((n_seq // 2,)),
            sem((2,)),
            pltpu.SemaphoreType.REGULAR,
        ],
        compiler_params=pltpu.CompilerParams(
            collective_id=0, has_side_effects=True, vmem_limit_bytes=48 * 1024 * 1024
        ),
        name="sparse_layer",
    )(*[pltpu.with_memory_space_constraint(x, pltpu.HBM) for x in operands])


def solution(mesh):
    placed = (P(("rep", "seq"), None), P(), P(), P(), P(), P(), P("rep"))
    return jax.shard_map(
        shards, mesh=mesh, in_specs=placed, out_specs=P(("rep", "seq"), None), check_vma=False
    )
```
